128 devices in a mesh: ctx: 32 (over z, x, core), head: 4 (over y).
Axes of the slice: x: 4, y: 4, z: 4, core: 2. Of those that a mesh axis runs over, the one named last changes fastest.
Arguments:
- queries: bfloat16 [16384, 2048], P('ctx', 'head'), may hold values from -6 to 6
- key_rows: bfloat16 [16384, 2048], P('ctx', 'head'), may hold values from -6 to 6
- value_rows: bfloat16 [16384, 2048], P('ctx', 'head'), may hold values from -6 to 6
- targets: bfloat16 [16384, 512], P('ctx'), may hold values from -2.5 to 2.5
- readout: bfloat16 [512, 4096], P(None, 'head'), may hold values from -0.25 to 0.25
- retain: float32 [32, 16], P('ctx', 'head'), may hold values from 0.3 to 1
- learn_rate: float32 [32, 16], P('ctx', 'head'), may hold values from 0.01 to 0.1
- allowed: int32 [32, 2], replicated, may hold values 0 or 1
- positions: int32 [32, 128], P('ctx'), may hold values from 0 to 511, as said below
- grad_out: bfloat16 [16384, 2048], P('ctx', 'head'), may hold values from -6 to 6
Outputs:
- grad_queries: float32 [16384, 2048], P('ctx', 'head')
- grad_keys: float32 [16384, 2048], P('ctx', 'head')
- grad_values: float32 [16384, 2048], P('ctx', 'head')
- grad_targets: float32 [16384, 512], P('ctx', 'head')
- grad_readout: float32 [512, 4096], P('ctx', 'head')
The draws below stay inside these ranges and needn't reach their ends.
Inputs may be any that keep to these rules, and one draw needn't show every extreme that they name: The 128 positions of a segment are distinct, ascending, and include 0 and 511.
All inputs are finite; a program needn't handle non-finite values.
Results may differ from the reference program's by a relative error of at most 0.0081.
Values may be sent and summed in bfloat16 or wider, within the bound.
A program may use at most 192 MiB of HBM per device.

```python
import math
import jax
import jax.numpy as jnp
from jax import lax

HEAD_COUNT = 16
DK = 128
FH = 512
SEG = 512
NM = 128
W = 2
D = 2048
SEGMENT_TOTAL = 32
TOKENS = 16384


def draw_retain(key, part):
    key_collection = jax.random.split(jax.random.fold_in(key, 31), 5)
    fast_count = HEAD_COUNT // 2
    head_order = jax.random.permutation(key_collection[0], HEAD_COUNT)
    slow_heads = (head_order >= fast_count)[None, :]
    spread = jax.random.uniform(key_collection[1], (SEGMENT_TOTAL, HEAD_COUNT), minval=0.3, maxval=1.5)
    gentle_learning_rate = jnp.exp(-spread / SEGMENT_TOTAL)
    fast_rate = jax.random.uniform(key_collection[2], (SEGMENT_TOTAL, HEAD_COUNT), minval=0.45, maxval=0.6)
    spike_row_count = jax.random.uniform(key_collection[3], (SEGMENT_TOTAL, 1)) < 3.0 / SEGMENT_TOTAL
    spike_multiplier = jax.random.uniform(key_collection[4], (SEGMENT_TOTAL, HEAD_COUNT), minval=0.5, maxval=0.8)
    gentle_value = gentle_learning_rate * jnp.where(spike_row_count, spike_multiplier, 1.0)
    return jnp.where(slow_heads, gentle_value, fast_rate).astype(jnp.float32)


def draw_positions(key, part):
    row_keys = jax.random.split(jax.random.fold_in(key, 17), SEGMENT_TOTAL)
    inner_rows = jax.vmap(lambda row_key: jax.random.permutation(row_key, SEG - 2))(row_keys)[:, :NM - 2] + 1
    first_column = jnp.zeros((SEGMENT_TOTAL, 1), jnp.int32)
    last_column = jnp.full((SEGMENT_TOTAL, 1), SEG - 1, jnp.int32)
    return jnp.sort(jnp.concatenate([first_column, inner_rows.astype(jnp.int32), last_column], axis=1), axis=1)


def drawn_rows(key, salt):
    return jnp.clip(jax.random.normal(jax.random.fold_in(key, salt), (TOKENS, D), jnp.float32), -6.0, 6.0)


def draw_queries(key, part):
    filled = drawn_rows(key, 1)
    return filled.astype(jnp.bfloat16)


def draw_key_rows(key, part):
    filled = drawn_rows(key, 2)
    return filled.astype(jnp.bfloat16)


def touch_ends(drawn, own_key, smallest, largest):
    longest = drawn.shape.index(max(drawn.shape))
    spots = []
    for shift in (0, 1):
        where = [jax.random.randint(jax.random.fold_in(own_key, axis), (), 0, length) for axis, length in enumerate(drawn.shape)]
        where[longest] = (where[longest] + shift) % drawn.shape[longest]
        spots.append(tuple(where))
    return drawn.at[spots[0]].set(smallest).at[spots[1]].set(largest)


def shard_levels(rng, shape, cuts, low, largest):
    gain, own = 1.0, jax.random.fold_in(rng, 6)
    for axis_at, shards_of in cuts:
        draws = jnp.exp(jax.random.uniform(jax.random.fold_in(own, axis_at), (shards_of,), jnp.float32, low / len(cuts), largest / len(cuts)))
        gain = gain * jnp.repeat(draws, shape[axis_at] // shards_of).reshape([-1 if axis == axis_at else 1 for axis in range(len(shape))])
    return gain


def normal_values(rng, extent, scale, reach, shards=(), kind=jnp.bfloat16):
    result = jax.random.normal(rng, extent, jnp.float32) * scale
    if len(shards) > 0:
        result = shard_levels(rng, extent, shards, -0.22, 0.18) * result
    return jnp.clip(result, min=-reach, max=reach).astype(kind)


def setup_inputs(seed: int = 0) -> dict:
    streams_of = jax.random.split(jax.random.key(seed), 11)
    return {
        "queries": draw_queries(jax.random.fold_in(streams_of[10], 71), 0),
        "key_rows": draw_key_rows(jax.random.fold_in(streams_of[10], 71), 0),
        "value_rows": normal_values(streams_of[2], (TOKENS, D), 1.0, 6.0, ((0, 32), (1, 4))),
        "targets": normal_values(streams_of[3], (TOKENS, FH), 0.3, 2.5, ((0, 32),)),
        "readout": normal_values(streams_of[4], (FH, 2 * D), FH ** -0.5, 0.25, ((1, 4),)),
        "retain": draw_retain(jax.random.fold_in(streams_of[10], 71), 0),
        "learn_rate": jnp.clip(jnp.exp(math.log(0.1) - 2.3025851 * jax.random.uniform(streams_of[6], (SEGMENT_TOTAL, HEAD_COUNT), jnp.float32) ** shard_levels(streams_of[6], (SEGMENT_TOTAL, HEAD_COUNT), ((0, 32), (1, 4)), -0.2, 0.2)), 0.01, 0.1),
        "allowed": touch_ends((jax.random.randint(streams_of[7], (SEGMENT_TOTAL, W), 0, 3) < 2).astype(jnp.int32), jax.random.fold_in(streams_of[7], 1), 0, 1),
        "positions": draw_positions(jax.random.fold_in(streams_of[10], 71), 0),
        "grad_out": normal_values(streams_of[9], (TOKENS, D), 1.0, 6.0, ((0, 32), (1, 4))),
    }


masked_score = -1.0e30
highest = lax.Precision.HIGHEST


def low_copy(values):
    return lax.optimization_barrier(values.astype(jnp.bfloat16)).astype(jnp.float32)


def reference(queries, key_rows, value_rows, targets, readout, retain, learn_rate, allowed, positions, grad_out):
    score_scale = DK ** -0.5
    query_segs = queries.reshape(SEGMENT_TOTAL, SEG, HEAD_COUNT, DK)
    key_segs = key_rows.reshape(SEGMENT_TOTAL, SEG, HEAD_COUNT, DK)
    value_segs = value_rows.reshape(SEGMENT_TOTAL, SEG, HEAD_COUNT, DK)
    cotangent_segs = grad_out.reshape(SEGMENT_TOTAL, SEG, HEAD_COUNT, DK)
    identity_block = jnp.eye(DK, dtype=jnp.float32)
    decay_maps = []
    states = [jnp.zeros((HEAD_COUNT, DK, FH), jnp.float32)]
    for segment in range(SEGMENT_TOTAL):
        keys_wide = key_segs[segment].astype(jnp.float32)
        target_wide = targets[segment * SEG:(segment + 1) * SEG].astype(jnp.float32)
        key_gram = jnp.einsum('sha,shb->hab', keys_wide, keys_wide, precision=highest)
        decay_map = retain[segment][:, None, None] * identity_block - (learn_rate[segment] / SEG)[:, None, None] * key_gram
        write_map = jnp.einsum('sha,sf->haf', keys_wide, target_wide, precision=highest) / SEG
        decay_maps.append(decay_map)
        states.append(jnp.einsum('hab,hbf->haf', decay_map, states[-1], precision=highest) + write_map)
    causal = jnp.arange(SEG)[:, None] >= jnp.arange(SEG)[None, :]
    key_acc = [jnp.zeros((SEG, HEAD_COUNT, DK), jnp.float32) for segment in range(SEGMENT_TOTAL)]
    value_acc = [jnp.zeros((SEG, HEAD_COUNT, DK), jnp.float32) for segment in range(SEGMENT_TOTAL)]
    query_acc = []
    grad_readout = jnp.zeros((FH, 2 * D), jnp.float32)
    grad_states = []
    for segment in range(SEGMENT_TOTAL):
        memory_in = states[segment]
        picked = query_segs[segment][positions[segment]].astype(jnp.float32)
        hidden_read = jnp.einsum('nha,haf->nf', picked, memory_in, precision=highest).astype(jnp.bfloat16)
        memory_tokens = jnp.dot(hidden_read, readout, preferred_element_type=jnp.float32).reshape(NM, HEAD_COUNT, 2, DK)
        key_parts = [memory_tokens[:, :, 0].astype(jnp.bfloat16), key_segs[segment]]
        value_parts = [memory_tokens[:, :, 1].astype(jnp.bfloat16), value_segs[segment]]
        mask_parts = [jnp.ones((SEG, NM), bool), causal]
        for offset in range(1, W + 1):
            source = segment - offset
            if source >= 0:
                key_parts.append(key_segs[source])
                value_parts.append(value_segs[source])
                mask_parts.append(jnp.broadcast_to(allowed[segment, offset - 1] == 1, (SEG, SEG)))
            else:
                key_parts.append(jnp.zeros((SEG, HEAD_COUNT, DK), jnp.bfloat16))
                value_parts.append(jnp.zeros((SEG, HEAD_COUNT, DK), jnp.bfloat16))
                mask_parts.append(jnp.zeros((SEG, SEG), bool))
        keys_all = jnp.concatenate(key_parts, 0).astype(jnp.float32)
        values_all = jnp.concatenate(value_parts, 0).astype(jnp.float32)
        mask_all = jnp.concatenate(mask_parts, 1)
        query_wide = query_segs[segment].astype(jnp.float32)
        cotangent_wide = cotangent_segs[segment].astype(jnp.float32)
        scores = jnp.einsum('ihd,jhd->hij', query_wide, keys_all, precision=highest) * score_scale
        scores = jnp.where(mask_all[None], scores, masked_score)
        exp_scores = jnp.exp(scores - jnp.max(scores, axis=2, keepdims=True))
        probs = exp_scores / jnp.sum(exp_scores, axis=2, keepdims=True)
        probs_low = low_copy(probs)
        attended = jnp.einsum('hij,jhd->hid', probs_low, values_all, precision=highest)
        row_delta = jnp.sum(jnp.transpose(cotangent_wide, (1, 0, 2)) * attended, axis=2, keepdims=True)
        grad_probs = jnp.einsum('ihd,jhd->hij', cotangent_wide, values_all, precision=highest)
        grad_scores = low_copy(probs * (grad_probs - row_delta))
        grad_query = jnp.einsum('hij,jhd->ihd', grad_scores, keys_all, precision=highest) * score_scale
        grad_key = jnp.einsum('hij,ihd->jhd', grad_scores, query_wide, precision=highest) * score_scale
        grad_value = jnp.einsum('hij,ihd->jhd', probs_low, cotangent_wide, precision=highest)
        key_acc[segment] = key_acc[segment] + grad_key[NM:NM + SEG]
        value_acc[segment] = value_acc[segment] + grad_value[NM:NM + SEG]
        for offset in range(1, W + 1):
            source = segment - offset
            if source >= 0:
                lower = NM + offset * SEG
                key_acc[source] = key_acc[source] + grad_key[lower:lower + SEG]
                value_acc[source] = value_acc[source] + grad_value[lower:lower + SEG]
        grad_memory = jnp.stack([grad_key[:NM], grad_value[:NM]], axis=2).reshape(NM, 2 * D).astype(jnp.bfloat16)
        grad_readout = grad_readout + jnp.dot(hidden_read.T, grad_memory, preferred_element_type=jnp.float32)
        grad_hidden = jnp.dot(grad_memory, readout.T, preferred_element_type=jnp.float32)
        grad_picked = jnp.einsum('nf,haf->nha', grad_hidden, memory_in, precision=highest)
        grad_states.append(jnp.einsum('nha,nf->haf', picked, grad_hidden, precision=highest))
        query_acc.append(grad_query.at[positions[segment]].add(grad_picked))
    carried = jnp.zeros((HEAD_COUNT, DK, FH), jnp.float32)
    grad_after = [None] * SEGMENT_TOTAL
    for segment in reversed(range(SEGMENT_TOTAL)):
        grad_after[segment] = carried
        carried = grad_states[segment] + jnp.einsum('hba,hbf->haf', decay_maps[segment], carried, precision=highest)
    target_list = []
    for segment in range(SEGMENT_TOTAL):
        keys_wide = key_segs[segment].astype(jnp.float32)
        target_wide = targets[segment * SEG:(segment + 1) * SEG].astype(jnp.float32)
        later_grad = grad_after[segment]
        grad_decay = jnp.einsum('haf,hbf->hab', later_grad, states[segment], precision=highest)
        symmetric = grad_decay + jnp.swapaxes(grad_decay, 1, 2)
        key_memory = jnp.einsum('sf,haf->sha', target_wide, later_grad, precision=highest) / SEG
        key_memory = key_memory - (learn_rate[segment] / SEG)[None, :, None] * jnp.einsum('sha,hab->shb', keys_wide, symmetric, precision=highest)
        key_acc[segment] = key_acc[segment] + key_memory
        target_list.append(jnp.einsum('sha,haf->sf', keys_wide, later_grad, precision=highest) / SEG)
    grad_queries = jnp.concatenate(query_acc, 0).reshape(TOKENS, D)
    grad_keys = jnp.concatenate(key_acc, 0).reshape(TOKENS, D)
    grad_values = jnp.concatenate(value_acc, 0).reshape(TOKENS, D)
    grad_targets = jnp.concatenate(target_list, 0)
    return grad_queries, grad_keys, grad_values, grad_targets, grad_readout
```

```python
import functools

import jax
import jax.numpy as jnp
from jax import lax
from jax.experimental import pallas as pl
from jax.experimental.pallas import tpu as pltpu
from jax.sharding import PartitionSpec as P

MESH = pl.DeviceIdType.MESH
BF = jnp.bfloat16
F32 = jnp.float32
NEG = -1e30
SEGS, HEADS, DK, FH, SEG, NM, PEERS = 32, 4, 128, 512, 512, 128, 4
WIDE = HEADS * DK
COLS = SEGS // HEADS
PIECE = FH // COLS
ROWS_R = 16
VM = pl.BlockSpec(memory_space=pltpu.VMEM)
SM = pl.BlockSpec(memory_space=pltpu.SMEM)
ANY = pl.BlockSpec(memory_space=pl.ANY)
LIMIT = 60 * 1024 * 1024


def nn(a, b):
    return lax.dot_general(a, b, (((1,), (0,)), ((), ())), preferred_element_type=F32)


def nt(a, b):
    return lax.dot_general(a, b, (((1,), (1,)), ((), ())), preferred_element_type=F32)


def tn(a, b):
    return lax.dot_general(a, b, (((0,), (0,)), ((), ())), preferred_element_type=F32)


def head(h):
    return slice(h * DK, (h + 1) * DK)


def prep_kernel(retain, rate, q, k, z, pos, er, bt, picked):
    onehot = (
        lax.broadcasted_iota(jnp.int32, (SEG, NM), 0) == pos[...]
    ).astype(F32).astype(BF)
    picked[...] = tn(onehot, q[...]).astype(BF)
    row = lax.broadcasted_iota(jnp.int32, (ROWS_R, DK), 0)
    for h in range(HEADS):
        kh = k[:, head(h)]
        er[h, 0:DK, :] = (tn(kh, kh) * (rate[0, h] / SEG)).astype(BF)
        whole = jnp.full((ROWS_R, DK), retain[0, h], F32)
        first = whole.astype(BF).astype(F32)
        second = (whole - first).astype(BF).astype(F32)
        third = whole - first - second
        er[h, DK:, :] = jnp.where(
            row == 0, first, jnp.where(row == 1, second, jnp.where(row == 2, third, 0.0))
        ).astype(BF)
        bt[h * COLS : (h + 1) * COLS] = (tn(z[...], kh) * (1.0 / SEG)).reshape(COLS, PIECE, DK)


def remote(src, dst, send, recv, where):
    return pltpu.make_async_remote_copy(
        src_ref=src, dst_ref=dst, send_sem=send, recv_sem=recv, device_id=where, device_id_type=MESH
    )


def enter(me, my):
    barrier = pltpu.get_barrier_semaphore()

    @pl.loop(1, SEGS)
    def _(d):
        pl.semaphore_signal(
            barrier, inc=1, device_id={"ctx": lax.rem(me + d, SEGS)}, device_id_type=MESH
        )

    for d in range(1, PEERS):
        pl.semaphore_signal(
            barrier, inc=1, device_id={"head": lax.rem(my + d, PEERS)}, device_id_type=MESH
        )
    pl.semaphore_wait(barrier, SEGS - 1 + PEERS - 1)


def retained(er_all, t):
    return jnp.sum(er_all[t, DK:, :].astype(F32), axis=0, keepdims=True)


def sum_over_heads(block, mine, landing, gathered, my, s_y, r_y):
    for d in range(PEERS):
        mine[d] = block(lax.rem(my + d, PEERS))

    def scatter(d):
        to = lax.rem(my + d, PEERS)
        return remote(mine.at[d], landing.at[d], s_y.at[d], r_y.at[d], {"head": to})

    def gather(d):
        to = lax.rem(my + d, PEERS)
        return remote(gathered.at[my], gathered.at[my], s_y.at[PEERS + d], r_y.at[PEERS + d], {"head": to})

    def started():
        for d in range(1, PEERS):
            scatter(d).start()

    def summed():
        total = mine[0]
        for d in range(1, PEERS):
            scatter(d).wait_recv()
            total = total + landing[d]
        gathered[my] = total.astype(BF)
        for d in range(1, PEERS):
            gather(d).start()

    def finished():
        for d in range(1, PEERS):
            src = lax.rem(my + PEERS - d, PEERS)
            remote(
                gathered.at[src], gathered.at[src], s_y.at[PEERS + d], r_y.at[PEERS + d], {"head": src}
            ).wait_recv()
        for d in range(1, PEERS):
            scatter(d).wait_send()
            gather(d).wait_send()
        return jnp.concatenate([gathered[j] for j in range(PEERS)], axis=1)

    return started, summed, finished


def forward_kernel(
    er, bt, kk, vv, qq, gg, picked, readout,
    er_out, mt_out, k1, v1, k2, v2, q1, g1, q2, g2, hid, tok,
    er_all, bt_all, outb, mt, mine_y, land_y, gath_y, part, state,
    s_er, r_er, s_bt, r_bt, s_m, r_m, s_halo, r_halo, s_y, r_y, loc,
):
    me, my = lax.axis_index("ctx"), lax.axis_index("head")
    mine = lax.div(me, COLS)
    core = lax.rem(me, 2)
    partner = me + 1 - 2 * core
    enter(me, my)

    def er_copy(to, src):
        return remote(er.at[lax.div(to, COLS)], er_all.at[src], s_er.at[to], r_er.at[src], {"ctx": to})

    def bt_copy(to, src):
        return remote(bt.at[to], bt_all.at[src], s_bt.at[to], r_bt.at[src], {"ctx": to})

    def m_copy(to, src):
        return remote(outb.at[to], mt.at[src], s_m.at[to], r_m.at[src], {"ctx": to})

    @pl.loop(1, SEGS)
    def _(d):
        to = lax.rem(me + d, SEGS)
        er_copy(to, me).start()
        bt_copy(to, me).start()

    def halo(src, dst, i, to):
        return remote(src, dst, s_halo.at[i], r_halo.at[i], {"ctx": to})

    after, before = lax.rem(me + 2, SEGS), lax.rem(me + SEGS - 2, SEGS)
    far = [
        halo(kk, k2, 0, after),
        halo(vv, v2, 1, after),
        halo(qq, q2, 2, before),
        halo(gg, g2, 3, before),
    ]
    keys_near = [halo(kk, k1, 4, partner), halo(vv, v1, 5, partner)]
    rows_near = [halo(qq, q1, 6, partner), halo(gg, g1, 7, partner)]
    keys_relay = [halo(k2, k1, 4, partner), halo(v2, v1, 5, partner)]
    rows_relay = [halo(q2, q1, 6, partner), halo(g2, g1, 7, partner)]
    for copy in far:
        copy.start()

    @pl.when(core == 0)
    def _():
        for copy in keys_near:
            copy.start()

    @pl.when(core == 1)
    def _():
        for copy in rows_near:
            copy.start()

    own_er = pltpu.make_async_copy(er.at[mine], er_all.at[me], loc.at[0])
    own_bt = pltpu.make_async_copy(bt.at[me], bt_all.at[me], loc.at[1])
    own_er.start()
    own_bt.start()
    own_er.wait()
    own_bt.wait()

    @pl.loop(1, SEGS)
    def _(d):
        src = lax.rem(me + SEGS - d, SEGS)
        er_copy(src, src).wait_recv()
        bt_copy(src, src).wait_recv()

    state[...] = jnp.zeros((PIECE, DK), F32)

    @pl.loop(0, SEGS)
    def _(t):
        old = state[...]
        outb[t] = old
        state[...] = retained(er_all, t) * old - nn(old.astype(BF), er_all[t, 0:DK, :]) + bt_all[t]

        @pl.when((t > 0) & (t - 1 != me))
        def _():
            m_copy(t - 1, me).start()

    @pl.when(me != SEGS - 1)
    def _():
        m_copy(SEGS - 1, me).start()

    own_m = pltpu.make_async_copy(outb.at[me], mt.at[me], loc.at[2])
    own_m.start()
    own_m.wait()

    @pl.loop(1, SEGS)
    def _(d):
        to = lax.rem(me + d, SEGS)
        er_copy(to, me).wait_send()
        bt_copy(to, me).wait_send()
        m_copy(to, me).wait_send()
        m_copy(to, to).wait_recv()

    for h in range(HEADS):
        m_h = mt[h * COLS : (h + 1) * COLS].reshape(FH, DK)
        high = m_h.astype(BF)
        low = (m_h - high.astype(F32)).astype(BF)
        mt_out[h * COLS : (h + 1) * COLS] = high.reshape(COLS, PIECE, DK)
        term = nt(picked[:, head(h)], high) + nt(picked[:, head(h)], low)
        for j in range(PEERS):
            if h == 0:
                part[j] = term[:, head(j)]
            else:
                part[j] += term[:, head(j)]
    started, summed, finished = sum_over_heads(lambda j: part[j], mine_y, land_y, gath_y, my, s_y, r_y)
    started()
    er_out[...] = er_all[...]
    summed()

    for copy in far:
        copy.wait_recv()

    @pl.when(core == 1)
    def _():
        for copy in keys_relay:
            copy.start()

    @pl.when(core == 0)
    def _():
        for copy in rows_relay:
            copy.start()

    low = finished()
    hid[...] = low
    tok[...] = nn(low, readout[...]).astype(BF)
    for copy in far:
        copy.wait_send()
    for copy in keys_near + rows_near:
        copy.wait()


def attention_kernel(allowed, q, g, k, v, k1, v1, k2, v2, tok, dq, dk, dv, gm, stats):
    scale = DK**-0.5
    segment = lax.axis_index("ctx")
    uses = [
        (allowed[segment, offset] == 1) & (segment > offset) for offset in range(2)
    ]
    q_t, g_t = q[...], g[...]
    causal = lax.broadcasted_iota(jnp.int32, (SEG, SEG), 0) >= lax.broadcasted_iota(
        jnp.int32, (SEG, SEG), 1
    )
    keys = [tok[:, 0:DK], k[...], k1[...], k2[...]]
    vals = [tok[:, DK:], v[...], v1[...], v2[...]]
    scores = [nt(q_t, key) for key in keys]
    scores[1] = jnp.where(causal, scores[1], NEG)
    scores[2] = jnp.where(uses[0], scores[2], NEG)
    scores[3] = jnp.where(uses[1], scores[3], NEG)
    top = functools.reduce(jnp.maximum, [jnp.max(s, axis=1, keepdims=True) for s in scores])
    exps = [jnp.exp((s - top) * scale) for s in scores]
    total = functools.reduce(jnp.add, [jnp.sum(e, axis=1, keepdims=True) for e in exps])
    inverse = 1.0 / total
    probs = [e * inverse for e in exps]
    lows = [p.astype(BF) for p in probs]
    attended = functools.reduce(jnp.add, [nn(p, value) for p, value in zip(lows, vals)])
    delta = jnp.sum(g_t.astype(F32) * attended, axis=1, keepdims=True)
    grads = [
        (p * (nt(g_t, value) - delta)).astype(BF) for p, value in zip(probs, vals)
    ]
    gm[:, 0:DK] = (tn(grads[0], q_t) * scale).astype(BF)
    gm[:, DK:] = tn(lows[0], g_t).astype(BF)
    dq[...] = functools.reduce(jnp.add, [nn(s, key) for s, key in zip(grads, keys)]) * scale
    dk[...] = tn(grads[1], q_t) * scale
    dv[...] = tn(lows[1], g_t)
    level = top * scale + jnp.log(total)
    lane = lax.broadcasted_iota(jnp.int32, (SEG, DK), 1)
    columns = jnp.where(
        lane == 0,
        jnp.where(uses[0], level, -NEG),
        jnp.where(lane == 1, jnp.where(uses[1], level, -NEG), delta),
    )
    stats[...] = columns.T[0:8, :]


def backward_kernel(
    rate, gm, readout, picked, hid, pos, stats, er_all_h, mt_h, kk_h, vv_h, zz_h, q1_h, g1_h, q2_h, g2_h,
    dq_h, dk_h, dv_h,
    out_q, out_k, out_v, out_z, out_r,
    er_all, mt, kk, vv, zz, q1, g1, q2, g2, dq, dk, dv,
    part, mine_y, land_y, gath_y, gsb, gs_all, gout, gt, rbuf, rall, tparts, st_in, state,
    s_gs, r_gs, s_g, r_g, s_r, r_r, s_y, r_y, s_t, r_t, s_st, r_st, loc, fetch,
):
    me, my = lax.axis_index("ctx"), lax.axis_index("head")
    scale = DK**-0.5
    fetched = [
        pltpu.make_async_copy(src, dst, fetch.at[i])
        for i, (src, dst) in enumerate(
            (
                (kk_h, kk), (vv_h, vv), (q1_h, q1), (g1_h, g1), (q2_h, q2), (g2_h, g2), (dk_h, dk), (dv_h, dv),
                (mt_h, mt), (dq_h, dq), (er_all_h, er_all), (zz_h, zz),
            )
        )
    ]
    for copy in fetched:
        copy.start()
    enter(me, my)

    def stat_copy(o):
        to = lax.rem(me + SEGS - o, SEGS)
        return remote(stats, st_in.at[o - 1], s_st.at[o - 1], r_st.at[o - 1], {"ctx": to})

    def gs_copy(to, src):
        return remote(gsb.at[to], gs_all.at[src], s_gs.at[to], r_gs.at[src], {"ctx": to})

    def g_copy(to, src):
        return remote(gout.at[to], gt.at[src], s_g.at[to], r_g.at[src], {"ctx": to})

    def r_copy(to, src):
        return remote(rbuf.at[to], rall.at[src], s_r.at[to], r_r.at[src], {"ctx": to})

    def far_tile(o, h):
        q_t, g_t = (q1, g1) if o == 1 else (q2, g2)
        q_t, g_t = q_t[:, head(h)], g_t[:, head(h)]
        level = st_in[o - 1, 8 * h + o - 1 : 8 * h + o, :]
        delta = st_in[o - 1, 8 * h + 2 : 8 * h + 3, :]
        probs = jnp.exp(nt(kk[:, head(h)], q_t) * scale - level)
        grads = probs * (nt(vv[:, head(h)], g_t) - delta)
        dv[:, head(h)] += nn(probs.astype(BF), g_t)
        dk[:, head(h)] += nn(grads.astype(BF), q_t) * scale

    term = nt(gm[...], readout[...])
    for j in range(PEERS):
        part[j] = term[:, head(j)]
    started, summed, finished = sum_over_heads(lambda j: part[j], mine_y, land_y, gath_y, my, s_y, r_y)
    started()
    for o in (1, 2):
        stat_copy(o).start()
    rbuf[...] = tn(hid[...], gm[...]).astype(BF).reshape(SEGS, FH // SEGS, 2 * WIDE)
    for copy in fetched[:8]:
        copy.wait()
    for o in (1, 2):
        stat_copy(o).wait()
    summed()
    far_tile(1, 0)
    far_tile(2, 0)
    gh = finished()

    for h in range(HEADS):
        gsb[h * COLS : (h + 1) * COLS] = (
            tn(gh, picked[:, head(h)]).astype(BF).reshape(COLS, PIECE, DK)
        )

    @pl.loop(1, SEGS)
    def _(d):
        gs_copy(lax.rem(me + d, SEGS), me).start()

    @pl.loop(1, SEGS)
    def _(d):
        r_copy(lax.rem(me + d, SEGS), me).start()

    own_gs = pltpu.make_async_copy(gsb.at[me], gs_all.at[me], loc.at[0])
    own_r = pltpu.make_async_copy(rbuf.at[me], rall.at[me], loc.at[1])
    own_gs.start()
    own_r.start()

    for h in range(1, HEADS):
        far_tile(1, h)
        far_tile(2, h)
    for copy in fetched[8:]:
        copy.wait()

    own_gs.wait()
    own_r.wait()

    @pl.loop(1, SEGS)
    def _(d):
        src = lax.rem(me + SEGS - d, SEGS)
        gs_copy(src, src).wait_recv()

    state[...] = jnp.zeros((PIECE, DK), F32)

    @pl.loop(0, SEGS)
    def _(i):
        t = SEGS - 1 - i
        old = state[...]
        low = old.astype(BF)
        gout[t] = low
        state[...] = retained(er_all, t) * old - nn(low, er_all[t, 0:DK, :]) + gs_all[t].astype(F32)

        @pl.when((i > 0) & (t + 1 != me))
        def _():
            g_copy(t + 1, me).start()

    @pl.when(me != 0)
    def _():
        g_copy(0, me).start()

    own_g = pltpu.make_async_copy(gout.at[me], gt.at[me], loc.at[2])
    own_g.start()

    onehot = (
        lax.broadcasted_iota(jnp.int32, (SEG, NM), 0) == pos[...]
    ).astype(F32).astype(BF)
    for h in range(HEADS):
        m_h = mt[h * COLS : (h + 1) * COLS].reshape(FH, DK)
        grad_picked = nn(gh, m_h).astype(BF)
        out_q[:, head(h)] = dq[:, head(h)] + nn(onehot, grad_picked)
    out_v[...] = dv[...]

    own_g.wait()

    @pl.loop(1, SEGS)
    def _(d):
        to = lax.rem(me + d, SEGS)
        gs_copy(to, me).wait_send()
        g_copy(to, me).wait_send()
        g_copy(to, to).wait_recv()

    term = jnp.zeros((SEG, FH), F32)
    for h in range(HEADS):
        g_h = gt[h * COLS : (h + 1) * COLS].reshape(FH, DK)
        term += nt(kk[:, head(h)], g_h)
    term = (term * (1.0 / SEG)).astype(BF)
    for j in range(PEERS):
        tparts[j] = term[:, head(j)]

    def t_copy(d):
        to = lax.rem(my + d, PEERS)
        return remote(tparts.at[to], tparts.at[PEERS + d], s_t.at[d], r_t.at[d], {"head": to})

    for d in range(1, PEERS):
        t_copy(d).start()

    for h in range(HEADS):
        g_h = gt[h * COLS : (h + 1) * COLS].reshape(FH, DK)
        m_h = mt[h * COLS : (h + 1) * COLS].reshape(FH, DK)
        both = (tn(g_h, m_h) + tn(m_h, g_h)).astype(BF)
        out_k[:, head(h)] = (
            dk[:, head(h)]
            + nn(zz[...], g_h) * (1.0 / SEG)
            - nn(kk[:, head(h)], both) * (rate[0, h] / SEG)
        )

    @pl.loop(1, SEGS)
    def _(d):
        to = lax.rem(me + d, SEGS)
        r_copy(to, me).wait_send()
        r_copy(to, to).wait_recv()

    out_r[...] = jnp.sum(rall[...].astype(F32), axis=0)

    for d in range(1, PEERS):
        t_copy(d).wait()
    grad = tparts[my].astype(F32)
    for d in range(1, PEERS):
        grad += tparts[PEERS + d].astype(F32)
    out_z[...] = grad


def shape(dims, kind):
    return jax.ShapeDtypeStruct(dims, kind)


def dma(*dims):
    return pltpu.SemaphoreType.DMA(dims)


def on_device(
    queries, key_rows, value_rows, targets, readout, retain, learn_rate, allowed, positions, grad_out
):
    block = (SEG, WIDE)
    er, bt, picked = pl.pallas_call(
        prep_kernel,
        out_shape=(
            shape((HEADS, DK + ROWS_R, DK), BF),
            shape((SEGS, PIECE, DK), F32),
            shape((NM, WIDE), BF),
        ),
        in_specs=[SM, SM, VM, VM, VM, VM],
        out_specs=(VM, VM, VM),
        name="prep",
    )(retain, learn_rate, queries, key_rows, targets, positions)

    sums = [
        pltpu.VMEM((PEERS, NM, FH // PEERS), F32),
        pltpu.VMEM((PEERS, NM, FH // PEERS), F32),
        pltpu.VMEM((PEERS, NM, FH // PEERS), BF),
    ]
    er_all, mt, k1, v1, k2, v2, q1, g1, q2, g2, hid, tok = pl.pallas_call(
        forward_kernel,
        out_shape=(
            shape((SEGS, DK + ROWS_R, DK), BF),
            shape((SEGS, PIECE, DK), BF),
        )
        + (shape(block, BF),) * 8
        + (
            shape((NM, FH), BF),
            shape((NM, 2 * WIDE), BF),
        ),
        in_specs=[VM, VM, ANY, ANY, ANY, ANY, VM, VM],
        out_specs=(VM, VM) + (ANY,) * 8 + (VM, VM),
        scratch_shapes=[
            pltpu.VMEM((SEGS, DK + ROWS_R, DK), BF),
            pltpu.VMEM((SEGS, PIECE, DK), F32),
            pltpu.VMEM((SEGS, PIECE, DK), F32),
            pltpu.VMEM((SEGS, PIECE, DK), F32),
        ]
        + sums
        + [
            pltpu.VMEM((PEERS, NM, FH // PEERS), F32),
            pltpu.VMEM((PIECE, DK), F32),
            dma(SEGS), dma(SEGS), dma(SEGS), dma(SEGS), dma(SEGS), dma(SEGS),
            dma(8), dma(8), dma(2 * PEERS), dma(2 * PEERS), dma(3),
        ],
        compiler_params=pltpu.CompilerParams(
            collective_id=0, has_side_effects=True, vmem_limit_bytes=LIMIT
        ),
        name="forward_scan",
    )(er, bt, key_rows, value_rows, queries, grad_out, picked, readout)

    one = pl.BlockSpec((SEG, DK), lambda h: (0, h))
    wide = pl.BlockSpec((NM, 2 * DK), lambda h: (0, h))
    dq, dk, dv, gm, stats = pl.pallas_call(
        attention_kernel,
        grid=(HEADS,),
        out_shape=(
            shape(block, F32),
            shape(block, F32),
            shape(block, F32),
            shape((NM, 2 * WIDE), BF),
            shape((8 * HEADS, SEG), F32),
        ),
        in_specs=[SM] + [one] * 8 + [wide],
        out_specs=(one,) * 3 + (wide, pl.BlockSpec((8, SEG), lambda h: (h, 0))),
        compiler_params=pltpu.CompilerParams(vmem_limit_bytes=LIMIT),
        name="attention",
    )(allowed, queries, grad_out, key_rows, value_rows, k1, v1, k2, v2, tok)

    return pl.pallas_call(
        backward_kernel,
        out_shape=(
            shape(block, F32),
            shape(block, F32),
            shape(block, F32),
            shape((SEG, FH // PEERS), F32),
            shape((FH // SEGS, 2 * WIDE), F32),
        ),
        in_specs=[SM] + [VM] * 6 + [ANY] * 12,
        out_specs=(VM,) * 5,
        scratch_shapes=[
            pltpu.VMEM((SEGS, DK + ROWS_R, DK), BF),
            pltpu.VMEM((SEGS, PIECE, DK), BF),
        ]
        + [pltpu.VMEM(block, BF)] * 7
        + [pltpu.VMEM(block, F32)] * 3
        + [pltpu.VMEM((PEERS, NM, FH // PEERS), F32)]
        + sums
        + [
            pltpu.VMEM((SEGS, PIECE, DK), BF),
            pltpu.VMEM((SEGS, PIECE, DK), BF),
            pltpu.VMEM((SEGS, PIECE, DK), BF),
            pltpu.VMEM((SEGS, PIECE, DK), BF),
            pltpu.VMEM((SEGS, FH // SEGS, 2 * WIDE), BF),
            pltpu.VMEM((SEGS, FH // SEGS, 2 * WIDE), BF),
            pltpu.VMEM((2 * PEERS, SEG, FH // PEERS), BF),
            pltpu.VMEM((2, 8 * HEADS, SEG), F32),
            pltpu.VMEM((PIECE, DK), F32),
            dma(SEGS), dma(SEGS), dma(SEGS), dma(SEGS), dma(SEGS), dma(SEGS),
            dma(2 * PEERS), dma(2 * PEERS), dma(PEERS), dma(PEERS), dma(2), dma(2), dma(3), dma(12),
        ],
        compiler_params=pltpu.CompilerParams(
            collective_id=1, has_side_effects=True, vmem_limit_bytes=LIMIT
        ),
        name="backward_scan",
    )(
        learn_rate, gm, readout, picked, hid, positions, stats, er_all, mt, key_rows, value_rows, targets,
        q1, g1, q2, g2, dq, dk, dv,
    )


def solution(mesh):
    return jax.shard_map(
        on_device,
        mesh=mesh,
        in_specs=(
            P("ctx", "head"),
            P("ctx", "head"),
            P("ctx", "head"),
            P("ctx", None),
            P(None, "head"),
            P("ctx", "head"),
            P("ctx", "head"),
            P(),
            P("ctx", None),
            P("ctx", "head"),
        ),
        out_specs=(P("ctx", "head"),) * 5,
        check_vma=False,
    )
```

```python
import functools

import jax
import jax.numpy as jnp
from jax import lax
from jax.experimental import pallas as pl
from jax.experimental.pallas import tpu as pltpu
from jax.sharding import PartitionSpec as P

MESH = pl.DeviceIdType.MESH
BF = jnp.bfloat16
F32 = jnp.float32
NEG = -1e30
STATE = F32
SEGS, HEADS, DK, FH, SEG, NM, PEERS = 32, 4, 128, 512, 512, 128, 4
WIDE = HEADS * DK
COLS = SEGS // HEADS
PIECE = FH // COLS
ROWS_R = 16
VM = pl.BlockSpec(memory_space=pltpu.VMEM)
SM = pl.BlockSpec(memory_space=pltpu.SMEM)
ANY = pl.BlockSpec(memory_space=pl.ANY)
LIMIT = 60 * 1024 * 1024


def nn(a, b):
    return lax.dot_general(a, b, (((1,), (0,)), ((), ())), preferred_element_type=F32)


def nt(a, b):
    return lax.dot_general(a, b, (((1,), (1,)), ((), ())), preferred_element_type=F32)


def tn(a, b):
    return lax.dot_general(a, b, (((0,), (0,)), ((), ())), preferred_element_type=F32)


def head(h):
    return slice(h * DK, (h + 1) * DK)


def prep_kernel(retain, rate, q, k, z, pos, er, bt, picked):
    onehot = (
        lax.broadcasted_iota(jnp.int32, (SEG, NM), 0) == pos[...]
    ).astype(F32).astype(BF)
    picked[...] = tn(onehot, q[...]).astype(BF)
    row = lax.broadcasted_iota(jnp.int32, (ROWS_R, DK), 0)
    for h in range(HEADS):
        kh = k[:, head(h)]
        er[h, 0:DK, :] = (tn(kh, kh) * (rate[0, h] / SEG)).astype(BF)
        whole = jnp.full((ROWS_R, DK), retain[0, h], F32)
        first = whole.astype(BF).astype(F32)
        second = (whole - first).astype(BF).astype(F32)
        third = whole - first - second
        er[h, DK:, :] = jnp.where(
            row == 0, first, jnp.where(row == 1, second, jnp.where(row == 2, third, 0.0))
        ).astype(BF)
        bt[h * COLS : (h + 1) * COLS] = (
            (tn(z[...], kh) * (1.0 / SEG)).astype(BF).reshape(COLS, PIECE, DK)
        )


def remote(src, dst, send, recv, where):
    return pltpu.make_async_remote_copy(
        src_ref=src, dst_ref=dst, send_sem=send, recv_sem=recv, device_id=where, device_id_type=MESH
    )


def enter(me, my):
    barrier = pltpu.get_barrier_semaphore()

    @pl.loop(1, SEGS)
    def _(d):
        pl.semaphore_signal(
            barrier, inc=1, device_id={"ctx": lax.rem(me + d, SEGS)}, device_id_type=MESH
        )

    for d in range(1, PEERS):
        pl.semaphore_signal(
            barrier, inc=1, device_id={"head": lax.rem(my + d, PEERS)}, device_id_type=MESH
        )
    pl.semaphore_wait(barrier, SEGS - 1 + PEERS - 1)


def place(dev):
    return lax.div(dev, 8), lax.rem(lax.div(dev, 2), 4), lax.rem(dev, 2)


def slot(dev):
    z, x, core = place(dev)
    return x * COLS + z * 2 + core


def er_slot(dev):
    z, x, core = place(dev)
    return core * 16 + z * 4 + x


def step(old, er_all, t, add):
    high = old.astype(BF)
    low = (old - high.astype(F32)).astype(BF)
    e = er_slot(t)
    decay = nn(jnp.concatenate([high, low], axis=0), er_all[e, 0:DK, :])
    share = jnp.sum(er_all[e, DK:, :].astype(F32), axis=0, keepdims=True)
    return share * old - (decay[:PIECE] + decay[PIECE:]) + add.astype(F32)


def sum_over_heads(block, mine, landing, gathered, my, s_y, r_y):
    for d in range(PEERS):
        mine[d] = block(lax.rem(my + d, PEERS))

    def scatter(d):
        to = lax.rem(my + d, PEERS)
        return remote(mine.at[d], landing.at[d], s_y.at[d], r_y.at[d], {"head": to})

    def gather(d):
        to = lax.rem(my + d, PEERS)
        return remote(gathered.at[my], gathered.at[my], s_y.at[PEERS + d], r_y.at[PEERS + d], {"head": to})

    def started():
        for d in range(1, PEERS):
            scatter(d).start()

    def summed():
        total = mine[0]
        for d in range(1, PEERS):
            scatter(d).wait_recv()
            total = total + landing[d]
        gathered[my] = total.astype(BF)
        for d in range(1, PEERS):
            gather(d).start()

    def finished():
        for d in range(1, PEERS):
            src = lax.rem(my + PEERS - d, PEERS)
            remote(
                gathered.at[src], gathered.at[src], s_y.at[PEERS + d], r_y.at[PEERS + d], {"head": src}
            ).wait_recv()
        for d in range(1, PEERS):
            scatter(d).wait_send()
            gather(d).wait_send()
        return jnp.concatenate([gathered[j] for j in range(PEERS)], axis=1)

    return started, summed, finished


def forward_kernel(
    er, bt, kk, vv, qq, gg, picked, readout,
    er_out, mt_out, k1, v1, k2, v2, q1, g1, q2, g2, hid, tok,
    er_all, bt_all, outb, mt, mine_y, land_y, gath_y, part, state,
    s_er, r_er, s_bt, r_bt, s_m, r_m, s_halo, r_halo, s_y, r_y, s_z, r_z, loc,
):
    me, my = lax.axis_index("ctx"), lax.axis_index("head")
    mz, mx, core = place(me)
    partner = me + 1 - 2 * core
    enter(me, my)

    def er_copy(x, to_x):
        return remote(
            er.at[to_x], er_all.at[core * 16 + mz * 4 + x], s_er.at[to_x], r_er.at[x],
            {"ctx": mz * 8 + to_x * 2 + core},
        )

    def block(side, z):
        return er_all.at[pl.ds(side * 16 + z * 4, 4)]

    def over_z(d):
        to = lax.rem(mz + d, 4)
        return remote(
            block(core, mz), block(core, mz), s_z.at[d], r_z.at[d], {"ctx": to * 8 + mx * 2 + core}
        )

    def over_core(d, side):
        z = lax.rem(mz + 4 - d, 4)
        return remote(block(side, z), block(side, z), s_z.at[4 + d], r_z.at[4 + d], {"ctx": partner})

    def bt_copy(to, src):
        return remote(bt.at[slot(to)], bt_all.at[src], s_bt.at[to], r_bt.at[src], {"ctx": to})

    def m_copy(to, src):
        return remote(outb.at[to], mt.at[slot(src)], s_m.at[to], r_m.at[src], {"ctx": to})

    for d in range(1, 4):
        er_copy(mx, lax.rem(mx + d, 4)).start()
    own_er = pltpu.make_async_copy(er.at[mx], er_all.at[er_slot(me)], loc.at[0])
    own_bt = pltpu.make_async_copy(bt.at[slot(me)], bt_all.at[me], loc.at[1])
    own_er.start()
    own_bt.start()

    @pl.loop(1, SEGS)
    def _(d):
        bt_copy(lax.rem(me + d, SEGS), me).start()

    def halo(src, dst, i, to):
        return remote(src, dst, s_halo.at[i], r_halo.at[i], {"ctx": to})

    after, before = lax.rem(me + 2, SEGS), lax.rem(me + SEGS - 2, SEGS)
    far = [
        halo(vv, v2, 0, after),
        halo(gg, g2, 1, before),
        halo(kk, k2, 2, after),
        halo(qq, q2, 3, before),
    ]
    keys_near = [halo(vv, v1, 4, partner), halo(kk, k1, 6, partner)]
    rows_near = [halo(gg, g1, 5, partner), halo(qq, q1, 7, partner)]
    keys_relay = [halo(v2, v1, 4, partner), halo(k2, k1, 6, partner)]
    rows_relay = [halo(g2, g1, 5, partner), halo(q2, q1, 7, partner)]
    for copy in far[:2]:
        copy.start()

    def relay(i):
        far[2 * i].wait_recv()
        far[2 * i + 1].wait_recv()

        @pl.when(core == 1)
        def _():
            keys_relay[i].start()

        @pl.when(core == 0)
        def _():
            rows_relay[i].start()

    own_er.wait()
    own_bt.wait()
    for d in range(1, 4):
        er_copy(lax.rem(mx + 4 - d, 4), mx).wait_recv()
    for d in range(1, 4):
        over_z(d).start()
    over_core(0, core).start()
    for d in range(1, 4):
        over_z(d).wait_recv()
        over_core(d, core).start()

    @pl.when(core == 0)
    def _():
        for copy in keys_near:
            copy.start()

    @pl.when(core == 1)
    def _():
        for copy in rows_near:
            copy.start()

    @pl.loop(1, SEGS)
    def _(d):
        src = lax.rem(me + SEGS - d, SEGS)
        bt_copy(src, src).wait_recv()

    for d in range(4):
        over_core(d, 1 - core).wait_recv()

    state[...] = jnp.zeros((PIECE, DK), F32)

    @pl.loop(0, SEGS)
    def _(t):
        old = state[...]
        outb[t] = old.astype(outb.dtype)
        state[...] = step(old, er_all, t, bt_all[t])

        @pl.when((t > 0) & (t - 1 != me))
        def _():
            m_copy(t - 1, me).start()

    @pl.when(me != SEGS - 1)
    def _():
        m_copy(SEGS - 1, me).start()

    own_m = pltpu.make_async_copy(outb.at[me], mt.at[slot(me)], loc.at[2])
    own_m.start()
    for copy in far[2:]:
        copy.start()
    er_out[...] = er_all[...]
    own_m.wait()

    @pl.loop(1, SEGS)
    def _(d):
        to = lax.rem(me + d, SEGS)
        bt_copy(to, me).wait_send()
        m_copy(to, me).wait_send()
        m_copy(to, to).wait_recv()

    for h in range(HEADS):
        m_h = mt[h * COLS : (h + 1) * COLS].reshape(FH, DK)
        high = m_h.astype(BF)
        mt_out[h * COLS : (h + 1) * COLS] = high.reshape(COLS, PIECE, DK)
        term = nt(picked[:, head(h)], high)
        if STATE == F32:
            term += nt(picked[:, head(h)], (m_h - high.astype(F32)).astype(BF))
        for j in range(PEERS):
            if h == 0:
                part[j] = term[:, head(j)]
            else:
                part[j] += term[:, head(j)]
    started, summed, finished = sum_over_heads(lambda j: part[j], mine_y, land_y, gath_y, my, s_y, r_y)
    started()
    relay(0)
    summed()
    low = finished()
    hid[...] = low
    tok[...] = nn(low, readout[...]).astype(BF)
    relay(1)
    for d in range(1, 4):
        er_copy(mx, lax.rem(mx + d, 4)).wait_send()
        over_z(d).wait_send()
    for d in range(4):
        over_core(d, core).wait_send()
    for copy in far:
        copy.wait_send()
    for copy in keys_near + rows_near:
        copy.wait()


def attention_kernel(allowed, q, g, k, v, k1, v1, k2, v2, tok, dq, dk, dv, gm, stats):
    scale = DK**-0.5
    segment = lax.axis_index("ctx")
    uses = [
        (allowed[0, offset] == 1) & (segment > offset) for offset in range(2)
    ]
    q_t, g_t = q[...], g[...]
    causal = lax.broadcasted_iota(jnp.int32, (SEG, SEG), 0) >= lax.broadcasted_iota(
        jnp.int32, (SEG, SEG), 1
    )
    keys = [tok[:, 0:DK], k[...], k1[...], k2[...]]
    vals = [tok[:, DK:], v[...], v1[...], v2[...]]
    scores = [nt(q_t, key) for key in keys]
    scores[1] = jnp.where(causal, scores[1], NEG)
    scores[2] = jnp.where(uses[0], scores[2], NEG)
    scores[3] = jnp.where(uses[1], scores[3], NEG)
    top = functools.reduce(jnp.maximum, [jnp.max(s, axis=1, keepdims=True) for s in scores])
    exps = [jnp.exp((s - top) * scale) for s in scores]
    total = functools.reduce(jnp.add, [jnp.sum(e, axis=1, keepdims=True) for e in exps])
    inverse = 1.0 / total
    probs = [e * inverse for e in exps]
    lows = [p.astype(BF) for p in probs]
    attended = functools.reduce(jnp.add, [nn(p, value) for p, value in zip(lows, vals)])
    delta = jnp.sum(g_t.astype(F32) * attended, axis=1, keepdims=True)
    grads = [
        (p * (nt(g_t, value) - delta)).astype(BF) for p, value in zip(probs, vals)
    ]
    gm[:, 0:DK] = (tn(grads[0], q_t) * scale).astype(BF)
    gm[:, DK:] = tn(lows[0], g_t).astype(BF)
    dq[...] = functools.reduce(jnp.add, [nn(s, key) for s, key in zip(grads, keys)]) * scale
    dk[...] = tn(grads[1], q_t) * scale
    dv[...] = tn(lows[1], g_t)
    level = top * scale + jnp.log(total)
    lane = lax.broadcasted_iota(jnp.int32, (SEG, DK), 1)
    columns = jnp.where(
        lane == 0,
        jnp.where(uses[0], level, -NEG),
        jnp.where(lane == 1, jnp.where(uses[1], level, -NEG), delta),
    )
    stats[...] = columns.T[0:8, :]


def backward_kernel(
    rate, gm, readout, picked, hid, pos, stats, er_all_h, mt_h, kk_h, vv_h, zz_h, q1_h, g1_h, q2_h, g2_h,
    dq_h, dk_h, dv_h,
    out_q, out_k, out_v, out_z, out_r,
    er_all, mt, kk, vv, zz, q1, g1, q2, g2, dq, dk, dv,
    part, mine_y, land_y, gath_y, gsb, gs_all, gout, gt, rterm, rlow, rpair, rbuf, rall, tparts, st_in, state,
    s_gs, r_gs, s_g, r_g, s_r, r_r, s_y, r_y, s_t, r_t, s_st, r_st, loc, fetch,
):
    me, my = lax.axis_index("ctx"), lax.axis_index("head")
    scale = DK**-0.5
    fetched = [
        pltpu.make_async_copy(src, dst, fetch.at[i])
        for i, (src, dst) in enumerate(
            (
                (kk_h, kk), (vv_h, vv), (q1_h, q1), (g1_h, g1), (q2_h, q2), (g2_h, g2), (dk_h, dk), (dv_h, dv),
                (mt_h, mt), (dq_h, dq), (er_all_h, er_all), (zz_h, zz),
            )
        )
    ]
    for copy in fetched:
        copy.start()
    enter(me, my)

    def stat_copy(o):
        to = lax.rem(me + SEGS - o, SEGS)
        return remote(stats, st_in.at[o - 1], s_st.at[o - 1], r_st.at[o - 1], {"ctx": to})

    def gs_copy(to, src):
        return remote(gsb.at[slot(to)], gs_all.at[src], s_gs.at[to], r_gs.at[src], {"ctx": to})

    def g_copy(to, src):
        return remote(gout.at[to], gt.at[slot(src)], s_g.at[to], r_g.at[src], {"ctx": to})

    core = lax.rem(me, 2)
    chip = lax.div(me, 2)
    pair = remote(rlow.at[1 - core], rpair, s_r.at[0], r_r.at[0], {"ctx": me + 1 - 2 * core})

    def r_copy(d):
        to = lax.rem(chip + d, SEGS // 2)
        return remote(rbuf.at[to], rall.at[chip], s_r.at[d], r_r.at[d], {"ctx": to * 2 + core})

    def far_tile(o, h):
        q_t, g_t = (q1, g1) if o == 1 else (q2, g2)
        q_t, g_t = q_t[:, head(h)], g_t[:, head(h)]
        level = st_in[o - 1, 8 * h + o - 1 : 8 * h + o, :]
        delta = st_in[o - 1, 8 * h + 2 : 8 * h + 3, :]
        probs = jnp.exp(nt(kk[:, head(h)], q_t) * scale - level)
        grads = probs * (nt(vv[:, head(h)], g_t) - delta)
        dv[:, head(h)] += nn(probs.astype(BF), g_t)
        dk[:, head(h)] += nn(grads.astype(BF), q_t) * scale

    term = nt(gm[...], readout[...])
    for j in range(PEERS):
        part[j] = term[:, head(j)]
    started, summed, finished = sum_over_heads(lambda j: part[j], mine_y, land_y, gath_y, my, s_y, r_y)
    started()
    for o in (1, 2):
        stat_copy(o).start()
    term = tn(hid[...], gm[...]).reshape(SEGS // 2, 2, FH // SEGS, 2 * WIDE)
    for side in range(2):
        rterm[side] = term[:, side]
        rlow[side] = term[:, side].astype(BF)
    pair.start()
    for copy in fetched[:8]:
        copy.wait()
    for o in (1, 2):
        stat_copy(o).wait()
    summed()
    far_tile(1, 0)
    far_tile(2, 0)
    gh = finished()

    for h in range(HEADS):
        gsb[h * COLS : (h + 1) * COLS] = (
            tn(gh, picked[:, head(h)]).astype(BF).reshape(COLS, PIECE, DK)
        )

    @pl.loop(1, SEGS)
    def _(d):
        gs_copy(lax.rem(me + d, SEGS), me).start()

    own_gs = pltpu.make_async_copy(gsb.at[slot(me)], gs_all.at[me], loc.at[0])
    pair.wait()
    rbuf[...] = (rterm[core] + rpair[...].astype(F32)).astype(BF)

    @pl.loop(1, SEGS // 2)
    def _(d):
        r_copy(d).start()

    own_r = pltpu.make_async_copy(rbuf.at[chip], rall.at[chip], loc.at[1])
    own_gs.start()
    own_r.start()

    for h in range(1, HEADS):
        far_tile(1, h)
        far_tile(2, h)
    for copy in fetched[8:]:
        copy.wait()

    own_gs.wait()
    own_r.wait()

    @pl.loop(1, SEGS)
    def _(d):
        src = lax.rem(me + SEGS - d, SEGS)
        gs_copy(src, src).wait_recv()

    state[...] = jnp.zeros((PIECE, DK), F32)

    @pl.loop(0, SEGS)
    def _(i):
        t = SEGS - 1 - i
        old = state[...]
        gout[t] = old.astype(BF)
        state[...] = step(old, er_all, t, gs_all[t])

        @pl.when((i > 0) & (t + 1 != me))
        def _():
            g_copy(t + 1, me).start()

    @pl.when(me != 0)
    def _():
        g_copy(0, me).start()

    own_g = pltpu.make_async_copy(gout.at[me], gt.at[slot(me)], loc.at[2])
    own_g.start()

    onehot = (
        lax.broadcasted_iota(jnp.int32, (SEG, NM), 0) == pos[...]
    ).astype(F32).astype(BF)
    for h in range(HEADS):
        m_h = mt[h * COLS : (h + 1) * COLS].reshape(FH, DK)
        grad_picked = nn(gh, m_h).astype(BF)
        out_q[:, head(h)] = dq[:, head(h)] + nn(onehot, grad_picked)
    out_v[...] = dv[...]

    own_g.wait()

    @pl.loop(1, SEGS)
    def _(d):
        to = lax.rem(me + d, SEGS)
        gs_copy(to, me).wait_send()
        g_copy(to, me).wait_send()
        g_copy(to, to).wait_recv()

    term = jnp.zeros((SEG, FH), F32)
    for h in range(HEADS):
        g_h = gt[h * COLS : (h + 1) * COLS].reshape(FH, DK)
        term += nt(kk[:, head(h)], g_h)
    term = (term * (1.0 / SEG)).astype(BF)
    for j in range(PEERS):
        tparts[j] = term[:, head(j)]

    def t_copy(d):
        to = lax.rem(my + d, PEERS)
        return remote(tparts.at[to], tparts.at[PEERS + d], s_t.at[d], r_t.at[d], {"head": to})

    for d in range(1, PEERS):
        t_copy(d).start()

    for h in range(HEADS):
        g_h = gt[h * COLS : (h + 1) * COLS].reshape(FH, DK)
        m_h = mt[h * COLS : (h + 1) * COLS].reshape(FH, DK)
        both = (tn(g_h, m_h) + tn(m_h, g_h)).astype(BF)
        out_k[:, head(h)] = (
            dk[:, head(h)]
            + nn(zz[...], g_h) * (1.0 / SEG)
            - nn(kk[:, head(h)], both) * (rate[0, h] / SEG)
        )

    @pl.loop(1, SEGS // 2)
    def _(d):
        r_copy(d).wait()

    out_r[...] = jnp.sum(rall[...].astype(F32), axis=0)

    for d in range(1, PEERS):
        t_copy(d).wait()
    grad = tparts[my].astype(F32)
    for d in range(1, PEERS):
        grad += tparts[PEERS + d].astype(F32)
    out_z[...] = grad


def finish_kernel(*refs):
    half = len(refs) // 2
    for src, dst in zip(refs[:half], refs[half:]):
        dst[...] = src[...]


def shape(dims, kind):
    return jax.ShapeDtypeStruct(dims, kind)


def dma(*dims):
    return pltpu.SemaphoreType.DMA(dims)


def on_device(
    queries, key_rows, value_rows, targets, readout, retain, learn_rate, allowed, positions, grad_out
):
    block = (SEG, WIDE)
    er, bt, picked = pl.pallas_call(
        prep_kernel,
        out_shape=(
            shape((HEADS, DK + ROWS_R, DK), BF),
            shape((SEGS, PIECE, DK), BF),
            shape((NM, WIDE), BF),
        ),
        in_specs=[SM, SM, VM, VM, VM, VM],
        out_specs=(VM, VM, VM),
        name="prep",
    )(retain, learn_rate, queries, key_rows, targets, positions)

    sums = [
        pltpu.VMEM((PEERS, NM, FH // PEERS), F32),
        pltpu.VMEM((PEERS, NM, FH // PEERS), F32),
        pltpu.VMEM((PEERS, NM, FH // PEERS), BF),
    ]
    er_all, mt, k1, v1, k2, v2, q1, g1, q2, g2, hid, tok = pl.pallas_call(
        forward_kernel,
        out_shape=(
            shape((SEGS, DK + ROWS_R, DK), BF),
            shape((SEGS, PIECE, DK), BF),
        )
        + (shape(block, BF),) * 8
        + (
            shape((NM, FH), BF),
            shape((NM, 2 * WIDE), BF),
        ),
        in_specs=[VM, VM, ANY, ANY, ANY, ANY, VM, VM],
        out_specs=(VM, VM) + (ANY,) * 8 + (VM, VM),
        scratch_shapes=[
            pltpu.VMEM((SEGS, DK + ROWS_R, DK), BF),
            pltpu.VMEM((SEGS, PIECE, DK), BF),
            pltpu.VMEM((SEGS, PIECE, DK), STATE),
            pltpu.VMEM((SEGS, PIECE, DK), STATE),
        ]
        + sums
        + [
            pltpu.VMEM((PEERS, NM, FH // PEERS), F32),
            pltpu.VMEM((PIECE, DK), F32),
            dma(4), dma(4), dma(SEGS), dma(SEGS), dma(SEGS), dma(SEGS),
            dma(8), dma(8), dma(2 * PEERS), dma(2 * PEERS), dma(8), dma(8), dma(3),
        ],
        compiler_params=pltpu.CompilerParams(
            collective_id=0, has_side_effects=True, vmem_limit_bytes=LIMIT
        ),
        name="forward_scan",
    )(er, bt, key_rows, value_rows, queries, grad_out, picked, readout)

    own_allowed = lax.dynamic_slice(allowed, (lax.axis_index("ctx"), 0), (1, 2))
    one = pl.BlockSpec((SEG, DK), lambda h: (0, h))
    wide = pl.BlockSpec((NM, 2 * DK), lambda h: (0, h))
    dq, dk, dv, gm, stats = pl.pallas_call(
        attention_kernel,
        grid=(HEADS,),
        out_shape=(
            shape(block, F32),
            shape(block, F32),
            shape(block, F32),
            shape((NM, 2 * WIDE), BF),
            shape((8 * HEADS, SEG), F32),
        ),
        in_specs=[SM] + [one] * 8 + [wide],
        out_specs=(one,) * 3 + (wide, pl.BlockSpec((8, SEG), lambda h: (h, 0))),
        compiler_params=pltpu.CompilerParams(vmem_limit_bytes=LIMIT),
        name="attention",
    )(own_allowed, queries, grad_out, key_rows, value_rows, k1, v1, k2, v2, tok)

    results = (
        shape(block, F32),
        shape(block, F32),
        shape(block, F32),
        shape((SEG, FH // PEERS), F32),
        shape((FH // SEGS, 2 * WIDE), F32),
    )
    outs = pl.pallas_call(
        backward_kernel,
        out_shape=results,
        in_specs=[SM] + [VM] * 6 + [ANY] * 12,
        out_specs=(VM,) * 5,
        scratch_shapes=[
            pltpu.VMEM((SEGS, DK + ROWS_R, DK), BF),
            pltpu.VMEM((SEGS, PIECE, DK), BF),
        ]
        + [pltpu.VMEM(block, BF)] * 7
        + [pltpu.VMEM(block, F32)] * 3
        + [pltpu.VMEM((PEERS, NM, FH // PEERS), F32)]
        + sums
        + [
            pltpu.VMEM((SEGS, PIECE, DK), BF),
            pltpu.VMEM((SEGS, PIECE, DK), BF),
            pltpu.VMEM((SEGS, PIECE, DK), BF),
            pltpu.VMEM((SEGS, PIECE, DK), BF),
            pltpu.VMEM((2, SEGS // 2, FH // SEGS, 2 * WIDE), F32),
            pltpu.VMEM((2, SEGS // 2, FH // SEGS, 2 * WIDE), BF),
            pltpu.VMEM((SEGS // 2, FH // SEGS, 2 * WIDE), BF),
            pltpu.VMEM((SEGS // 2, FH // SEGS, 2 * WIDE), BF),
            pltpu.VMEM((SEGS // 2, FH // SEGS, 2 * WIDE), BF),
            pltpu.VMEM((2 * PEERS, SEG, FH // PEERS), BF),
            pltpu.VMEM((2, 8 * HEADS, SEG), F32),
            pltpu.VMEM((PIECE, DK), F32),
            dma(SEGS), dma(SEGS), dma(SEGS), dma(SEGS), dma(SEGS // 2), dma(SEGS // 2),
            dma(2 * PEERS), dma(2 * PEERS), dma(PEERS), dma(PEERS), dma(2), dma(2), dma(3), dma(12),
        ],
        compiler_params=pltpu.CompilerParams(
            collective_id=1, has_side_effects=True, vmem_limit_bytes=LIMIT
        ),
        name="backward_scan",
    )(
        learn_rate, gm, readout, picked, hid, positions, stats, er_all, mt, key_rows, value_rows, targets,
        q1, g1, q2, g2, dq, dk, dv,
    )
    specs = (
        (one,) * 3
        + (pl.BlockSpec((SEG // HEADS, FH // PEERS), lambda h: (h, 0)),)
        + (pl.BlockSpec((FH // SEGS, 2 * DK), lambda h: (0, h)),)
    )
    return pl.pallas_call(
        finish_kernel, grid=(HEADS,), out_shape=results, in_specs=list(specs), out_specs=specs, name="finish"
    )(*outs)


def solution(mesh):
    return jax.shard_map(
        on_device,
        mesh=mesh,
        in_specs=(
            P("ctx", "head"),
            P("ctx", "head"),
            P("ctx", "head"),
            P("ctx", None),
            P(None, "head"),
            P("ctx", "head"),
            P("ctx", "head"),
            P(),
            P("ctx", None),
            P("ctx", "head"),
        ),
        out_specs=(P("ctx", "head"),) * 5,
        check_vma=False,
    )
```

```python
import functools

import jax
import jax.numpy as jnp
from jax import lax
from jax.experimental import pallas as pl
from jax.experimental.pallas import tpu as pltpu
from jax.sharding import PartitionSpec as P

MESH = pl.DeviceIdType.MESH
BF = jnp.bfloat16
F32 = jnp.float32
NEG = -1e30
STATE = F32
SEGS, HEADS, DK, FH, SEG, NM, PEERS = 32, 4, 128, 512, 512, 128, 4
WIDE = HEADS * DK
COLS = SEGS // HEADS
PIECE = FH // COLS
ROWS_R = 16
VM = pl.BlockSpec(memory_space=pltpu.VMEM)
SM = pl.BlockSpec(memory_space=pltpu.SMEM)
ANY = pl.BlockSpec(memory_space=pl.ANY)
LIMIT = 60 * 1024 * 1024


def nn(a, b):
    return lax.dot_general(a, b, (((1,), (0,)), ((), ())), preferred_element_type=F32)


def nt(a, b):
    return lax.dot_general(a, b, (((1,), (1,)), ((), ())), preferred_element_type=F32)


def tn(a, b):
    return lax.dot_general(a, b, (((0,), (0,)), ((), ())), preferred_element_type=F32)


def head(h):
    return slice(h * DK, (h + 1) * DK)


def local_maps(retain, rate, q, k, z, pos, er, bt, picked):
    onehot = (
        lax.broadcasted_iota(jnp.int32, (SEG, NM), 0) == pos[...]
    ).astype(F32).astype(BF)
    row = lax.broadcasted_iota(jnp.int32, (ROWS_R, DK), 0)
    for h in range(HEADS):
        kh = k[:, head(h)]
        er[h, 0:DK, :] = (tn(kh, kh) * (rate[0, h] / SEG)).astype(BF)
        whole = jnp.full((ROWS_R, DK), retain[0, h], F32)
        first = whole.astype(BF).astype(F32)
        second = (whole - first).astype(BF).astype(F32)
        third = whole - first - second
        er[h, DK:, :] = jnp.where(
            row == 0, first, jnp.where(row == 1, second, jnp.where(row == 2, third, 0.0))
        ).astype(BF)
    for h in range(HEADS):
        bt[h * COLS : (h + 1) * COLS] = (
            (tn(z[...], k[:, head(h)]) * (1.0 / SEG)).astype(BF).reshape(COLS, PIECE, DK)
        )
    picked[...] = tn(onehot, q[...]).astype(BF)


def remote(src, dst, send, recv, where):
    return pltpu.make_async_remote_copy(
        src_ref=src, dst_ref=dst, send_sem=send, recv_sem=recv, device_id=where, device_id_type=MESH
    )


def greet(me, my):
    barrier = pltpu.get_barrier_semaphore()

    @pl.loop(1, SEGS)
    def _(d):
        pl.semaphore_signal(
            barrier, inc=1, device_id={"ctx": lax.rem(me + d, SEGS)}, device_id_type=MESH
        )

    for d in range(1, PEERS):
        pl.semaphore_signal(
            barrier, inc=1, device_id={"head": lax.rem(my + d, PEERS)}, device_id_type=MESH
        )
    return lambda: pl.semaphore_wait(barrier, SEGS - 1 + PEERS - 1)


def place(dev):
    return lax.div(dev, 8), lax.rem(lax.div(dev, 2), 4), lax.rem(dev, 2)


def slot(dev):
    z, x, core = place(dev)
    return x * COLS + z * 2 + core


def er_slot(dev):
    z, x, core = place(dev)
    return core * 16 + z * 4 + x


def step(old, er_all, t, add):
    high = old.astype(BF)
    low = (old - high.astype(F32)).astype(BF)
    e = er_slot(t)
    decay = nn(jnp.concatenate([high, low], axis=0), er_all[e, 0:DK, :])
    share = jnp.sum(er_all[e, DK:, :].astype(F32), axis=0, keepdims=True)
    return share * old - (decay[:PIECE] + decay[PIECE:]) + add.astype(F32)


def sum_over_heads(block, mine, landing, gathered, my, s_y, r_y):
    for d in range(PEERS):
        mine[d] = block(lax.rem(my + d, PEERS))

    def scatter(d):
        to = lax.rem(my + d, PEERS)
        return remote(mine.at[d], landing.at[d], s_y.at[d], r_y.at[d], {"head": to})

    def gather(d):
        to = lax.rem(my + d, PEERS)
        return remote(gathered.at[my], gathered.at[my], s_y.at[PEERS + d], r_y.at[PEERS + d], {"head": to})

    def started():
        for d in range(1, PEERS):
            scatter(d).start()

    def summed():
        total = mine[0]
        for d in range(1, PEERS):
            scatter(d).wait_recv()
            total = total + landing[d]
        gathered[my] = total.astype(BF)
        for d in range(1, PEERS):
            gather(d).start()

    def finished():
        for d in range(1, PEERS):
            src = lax.rem(my + PEERS - d, PEERS)
            remote(
                gathered.at[src], gathered.at[src], s_y.at[PEERS + d], r_y.at[PEERS + d], {"head": src}
            ).wait_recv()
        for d in range(1, PEERS):
            scatter(d).wait_send()
            gather(d).wait_send()
        return jnp.concatenate([gathered[j] for j in range(PEERS)], axis=1)

    return started, summed, finished


def forward_kernel(
    retain, rate, q, k, z, pos, kk, vv, qq, gg, readout,
    er_out, mt_out, k1, v1, k2, v2, q1, g1, q2, g2, hid, tok, picked,
    er, bt, er_all, bt_all, outb, mt, mine_y, land_y, gath_y, part, state,
    s_er, r_er, s_bt, r_bt, s_m, r_m, s_halo, r_halo, s_y, r_y, s_z, r_z, loc,
):
    me, my = lax.axis_index("ctx"), lax.axis_index("head")
    mz, mx, core = place(me)
    partner = me + 1 - 2 * core
    entered = greet(me, my)
    local_maps(retain, rate, q, k, z, pos, er, bt, picked)
    entered()

    def er_copy(x, to_x):
        return remote(
            er.at[to_x], er_all.at[core * 16 + mz * 4 + x], s_er.at[to_x], r_er.at[x],
            {"ctx": mz * 8 + to_x * 2 + core},
        )

    def block(side, z):
        return er_all.at[pl.ds(side * 16 + z * 4, 4)]

    def over_z(d):
        to = lax.rem(mz + d, 4)
        return remote(
            block(core, mz), block(core, mz), s_z.at[d], r_z.at[d], {"ctx": to * 8 + mx * 2 + core}
        )

    def over_core(d, side):
        z = lax.rem(mz + 4 - d, 4)
        return remote(block(side, z), block(side, z), s_z.at[4 + d], r_z.at[4 + d], {"ctx": partner})

    def bt_copy(to, src):
        return remote(bt.at[slot(to)], bt_all.at[src], s_bt.at[to], r_bt.at[src], {"ctx": to})

    def m_copy(to, src):
        return remote(outb.at[to], mt.at[slot(src)], s_m.at[to], r_m.at[src], {"ctx": to})

    for d in range(1, 4):
        er_copy(mx, lax.rem(mx + d, 4)).start()
    own_er = pltpu.make_async_copy(er.at[mx], er_all.at[er_slot(me)], loc.at[0])
    own_bt = pltpu.make_async_copy(bt.at[slot(me)], bt_all.at[me], loc.at[1])
    own_er.start()
    own_bt.start()

    @pl.loop(1, SEGS)
    def _(d):
        bt_copy(lax.rem(me + d, SEGS), me).start()

    def halo(src, dst, i, to):
        return remote(src, dst, s_halo.at[i], r_halo.at[i], {"ctx": to})

    after, before = lax.rem(me + 2, SEGS), lax.rem(me + SEGS - 2, SEGS)
    far = [
        halo(vv, v2, 0, after),
        halo(gg, g2, 1, before),
        halo(kk, k2, 2, after),
        halo(qq, q2, 3, before),
    ]
    keys_near = [halo(vv, v1, 4, partner), halo(kk, k1, 6, partner)]
    rows_near = [halo(gg, g1, 5, partner), halo(qq, q1, 7, partner)]
    keys_relay = [halo(v2, v1, 4, partner), halo(k2, k1, 6, partner)]
    rows_relay = [halo(g2, g1, 5, partner), halo(q2, q1, 7, partner)]
    for copy in far[:2]:
        copy.start()

    def relay(i):
        far[2 * i].wait_recv()
        far[2 * i + 1].wait_recv()

        @pl.when(core == 1)
        def _():
            keys_relay[i].start()

        @pl.when(core == 0)
        def _():
            rows_relay[i].start()

    own_er.wait()
    own_bt.wait()
    for d in range(1, 4):
        er_copy(lax.rem(mx + 4 - d, 4), mx).wait_recv()
    for d in range(1, 4):
        over_z(d).start()
    over_core(0, core).start()
    for d in range(1, 4):
        over_z(d).wait_recv()
        over_core(d, core).start()

    @pl.when(core == 0)
    def _():
        for copy in keys_near:
            copy.start()

    @pl.when(core == 1)
    def _():
        for copy in rows_near:
            copy.start()

    @pl.loop(1, SEGS)
    def _(d):
        src = lax.rem(me + SEGS - d, SEGS)
        bt_copy(src, src).wait_recv()

    for d in range(4):
        over_core(d, 1 - core).wait_recv()

    state[...] = jnp.zeros((PIECE, DK), F32)

    @pl.loop(0, SEGS)
    def _(t):
        old = state[...]
        outb[t] = old.astype(outb.dtype)
        state[...] = step(old, er_all, t, bt_all[t])

        @pl.when((t > 0) & (t - 1 != me))
        def _():
            m_copy(t - 1, me).start()

    @pl.when(me != SEGS - 1)
    def _():
        m_copy(SEGS - 1, me).start()

    own_m = pltpu.make_async_copy(outb.at[me], mt.at[slot(me)], loc.at[2])
    own_m.start()
    er_out[...] = er_all[...]
    own_m.wait()

    @pl.loop(1, SEGS)
    def _(d):
        to = lax.rem(me + d, SEGS)
        bt_copy(to, me).wait_send()
        m_copy(to, me).wait_send()
        m_copy(to, to).wait_recv()

    for copy in far[2:]:
        copy.start()
    for h in range(HEADS):
        m_h = mt[h * COLS : (h + 1) * COLS].reshape(FH, DK)
        high = m_h.astype(BF)
        mt_out[h * COLS : (h + 1) * COLS] = high.reshape(COLS, PIECE, DK)
        term = nt(picked[:, head(h)], high)
        if STATE == F32:
            term += nt(picked[:, head(h)], (m_h - high.astype(F32)).astype(BF))
        for j in range(PEERS):
            if h == 0:
                part[j] = term[:, head(j)]
            else:
                part[j] += term[:, head(j)]
    started, summed, finished = sum_over_heads(lambda j: part[j], mine_y, land_y, gath_y, my, s_y, r_y)
    started()
    relay(0)
    summed()
    low = finished()
    hid[...] = low
    tok[...] = nn(low, readout[...]).astype(BF)
    relay(1)
    for d in range(1, 4):
        er_copy(mx, lax.rem(mx + d, 4)).wait_send()
        over_z(d).wait_send()
    for d in range(4):
        over_core(d, core).wait_send()
    for copy in far:
        copy.wait_send()
    for copy in keys_near + rows_near:
        copy.wait()


def backward_kernel(
    rate, bias, tok, readout, picked, hid, pos,
    q_h, g_h, k_h, v_h, k1_h, v1_h, k2_h, v2_h, q1_h, g1_h, q2_h, g2_h, mt_h, er_all_h, zz_h,
    out_q, out_k, out_v, out_z, out_r,
    qq, gg, kk, vv, k1, v1, k2, v2, q1, g1, q2, g2, mt, er_all, zz,
    gm, stats, scores_grad, own_probs,
    part, mine_y, land_y, gath_y, gsb, gs_all, gout, gt, rterm, rlow, rpair, rbuf, rall, tparts, st_in, state,
    s_gs, r_gs, s_g, r_g, s_r, r_r, s_y, r_y, s_t, r_t, s_st, r_st, loc, fetch,
):
    me, my = lax.axis_index("ctx"), lax.axis_index("head")
    scale = DK**-0.5
    entered = greet(me, my)
    fetched = [
        pltpu.make_async_copy(src, dst, fetch.at[i])
        for i, (src, dst) in enumerate(
            (
                (q_h, qq), (k_h, kk), (k1_h, k1), (k2_h, k2), (v_h, vv), (v1_h, v1), (v2_h, v2), (g_h, gg),
                (q1_h, q1), (g1_h, g1), (q2_h, q2), (g2_h, g2), (mt_h, mt), (er_all_h, er_all), (zz_h, zz),
            )
        )
    ]
    for copy in fetched:
        copy.start()
    for copy in fetched[:8]:
        copy.wait()

    @pl.loop(0, HEADS)
    def _(h):
        lanes = pl.ds(pl.multiple_of(h * DK, DK), DK)
        tok_k = pl.ds(pl.multiple_of(h * 2 * DK, DK), DK)
        tok_v = pl.ds(pl.multiple_of(h * 2 * DK + DK, DK), DK)
        q_t, g_t = qq[:, lanes], gg[:, lanes]
        causal = lax.broadcasted_iota(jnp.int32, (SEG, SEG), 0) >= lax.broadcasted_iota(
            jnp.int32, (SEG, SEG), 1
        )
        keys = [kk[:, lanes], k1[:, lanes], k2[:, lanes], tok[:, tok_k]]
        vals = [vv[:, lanes], v1[:, lanes], v2[:, lanes], tok[:, tok_v]]
        scores = [nt(q_t, key) for key in keys]
        scores[0] = jnp.where(causal, scores[0], NEG)
        scores[1] = scores[1] + bias[0, 0]
        scores[2] = scores[2] + bias[0, 1]
        top = functools.reduce(jnp.maximum, [jnp.max(s, axis=1, keepdims=True) for s in scores])
        exps = [jnp.exp((s - top) * scale) for s in scores]
        total = functools.reduce(jnp.add, [jnp.sum(e, axis=1, keepdims=True) for e in exps])
        inverse = 1.0 / total
        probs = [e * inverse for e in exps]
        lows = [p.astype(BF) for p in probs]
        attended = functools.reduce(jnp.add, [nn(p, value) for p, value in zip(lows, vals)])
        delta = jnp.sum(g_t.astype(F32) * attended, axis=1, keepdims=True)
        grads = [
            (p * (nt(g_t, value) - delta)).astype(BF) for p, value in zip(probs, vals)
        ]
        gm[:, tok_k] = (tn(grads[3], q_t) * scale).astype(BF)
        gm[:, tok_v] = tn(lows[3], g_t).astype(BF)
        own_probs[h] = lows[0]
        for i in range(3):
            scores_grad[h, :, i * SEG : (i + 1) * SEG] = grads[i]
        scores_grad[h, :, 3 * SEG :] = grads[3]
        level = top * scale + jnp.log(total)
        lane = lax.broadcasted_iota(jnp.int32, (SEG, DK), 1)
        columns = jnp.where(
            lane == 0, level - bias[0, 0], jnp.where(lane == 1, level - bias[0, 1], delta)
        )
        stats[pl.ds(pl.multiple_of(h * 8, 8), 8), :] = columns.T[0:8, :]

    entered()

    def stat_copy(o):
        to = lax.rem(me + SEGS - o, SEGS)
        return remote(stats, st_in.at[o - 1], s_st.at[o - 1], r_st.at[o - 1], {"ctx": to})

    def gs_copy(to, src):
        return remote(gsb.at[slot(to)], gs_all.at[src], s_gs.at[to], r_gs.at[src], {"ctx": to})

    def g_copy(to, src):
        return remote(gout.at[to], gt.at[slot(src)], s_g.at[to], r_g.at[src], {"ctx": to})

    core = lax.rem(me, 2)
    chip = lax.div(me, 2)
    pair = remote(rlow.at[1 - core], rpair, s_r.at[0], r_r.at[0], {"ctx": me + 1 - 2 * core})

    def r_copy(d):
        to = lax.rem(chip + d, SEGS // 2)
        return remote(rbuf.at[to], rall.at[chip], s_r.at[d], r_r.at[d], {"ctx": to * 2 + core})

    def own_tile(h):
        grad = scores_grad[h, :, 0:SEG]
        out_q[:, head(h)] = (
            nn(grad, kk[:, head(h)])
            + nn(scores_grad[h, :, SEG : 2 * SEG], k1[:, head(h)])
            + nn(scores_grad[h, :, 2 * SEG : 3 * SEG], k2[:, head(h)])
            + nn(scores_grad[h, :, 3 * SEG :], tok[:, 2 * h * DK : (2 * h + 1) * DK])
        ) * scale
        out_k[:, head(h)] = tn(grad, qq[:, head(h)]) * scale
        out_v[:, head(h)] = tn(own_probs[h], gg[:, head(h)])

    def far_tile(o, h):
        q_t, g_t = (q1, g1) if o == 1 else (q2, g2)
        q_t, g_t = q_t[:, head(h)], g_t[:, head(h)]
        level = st_in[o - 1, 8 * h + o - 1 : 8 * h + o, :]
        delta = st_in[o - 1, 8 * h + 2 : 8 * h + 3, :]
        probs = jnp.exp(nt(kk[:, head(h)], q_t) * scale - level)
        grads = probs * (nt(vv[:, head(h)], g_t) - delta)
        out_v[:, head(h)] += nn(probs.astype(BF), g_t)
        out_k[:, head(h)] += nn(grads.astype(BF), q_t) * scale

    term = nt(gm[...], readout[...])
    for j in range(PEERS):
        part[j] = term[:, head(j)]
    started, summed, finished = sum_over_heads(lambda j: part[j], mine_y, land_y, gath_y, my, s_y, r_y)
    started()
    for o in (1, 2):
        stat_copy(o).start()
    term = tn(hid[...], gm[...]).reshape(SEGS // 2, 2, FH // SEGS, 2 * WIDE)
    for side in range(2):
        rterm[side] = term[:, side]
        rlow[side] = term[:, side].astype(BF)
    pair.start()
    own_tile(0)
    own_tile(1)
    summed()
    own_tile(2)
    own_tile(3)
    gh = finished()

    for h in range(HEADS):
        gsb[h * COLS : (h + 1) * COLS] = (
            tn(gh, picked[:, head(h)]).astype(BF).reshape(COLS, PIECE, DK)
        )

    @pl.loop(1, SEGS)
    def _(d):
        gs_copy(lax.rem(me + d, SEGS), me).start()

    own_gs = pltpu.make_async_copy(gsb.at[slot(me)], gs_all.at[me], loc.at[0])
    own_gs.start()
    for o in (1, 2):
        stat_copy(o).wait()
    for copy in fetched[8:]:
        copy.wait()
    far_tile(1, 0)
    far_tile(2, 0)
    pair.wait()
    rbuf[...] = (rterm[core] + rpair[...].astype(F32)).astype(BF)
    far_tile(1, 1)

    @pl.loop(1, SEGS // 2)
    def _(d):
        r_copy(d).start()

    own_r = pltpu.make_async_copy(rbuf.at[chip], rall.at[chip], loc.at[1])
    own_r.start()
    far_tile(2, 1)
    far_tile(1, 2)
    far_tile(2, 2)

    own_gs.wait()
    own_r.wait()

    @pl.loop(1, SEGS)
    def _(d):
        src = lax.rem(me + SEGS - d, SEGS)
        gs_copy(src, src).wait_recv()

    state[...] = jnp.zeros((PIECE, DK), F32)

    @pl.loop(0, SEGS)
    def _(i):
        t = SEGS - 1 - i
        old = state[...]
        gout[t] = old.astype(BF)
        state[...] = step(old, er_all, t, gs_all[t])

        @pl.when((i > 0) & (t + 1 != me))
        def _():
            g_copy(t + 1, me).start()

    @pl.when(me != 0)
    def _():
        g_copy(0, me).start()

    own_g = pltpu.make_async_copy(gout.at[me], gt.at[slot(me)], loc.at[2])
    own_g.start()
    far_tile(1, 3)
    far_tile(2, 3)

    onehot = (
        lax.broadcasted_iota(jnp.int32, (SEG, NM), 0) == pos[...]
    ).astype(F32).astype(BF)
    for h in range(HEADS):
        m_h = mt[h * COLS : (h + 1) * COLS].reshape(FH, DK)
        grad_picked = nn(gh, m_h).astype(BF)
        out_q[:, head(h)] += nn(onehot, grad_picked)

    own_g.wait()

    @pl.loop(1, SEGS)
    def _(d):
        to = lax.rem(me + d, SEGS)
        gs_copy(to, me).wait_send()
        g_copy(to, me).wait_send()
        g_copy(to, to).wait_recv()

    term = jnp.zeros((SEG, FH), F32)
    for h in range(HEADS):
        g_h = gt[h * COLS : (h + 1) * COLS].reshape(FH, DK)
        term += nt(kk[:, head(h)], g_h)
    term = (term * (1.0 / SEG)).astype(BF)
    for j in range(PEERS):
        tparts[j] = term[:, head(j)]

    def t_copy(d):
        to = lax.rem(my + d, PEERS)
        return remote(tparts.at[to], tparts.at[PEERS + d], s_t.at[d], r_t.at[d], {"head": to})

    for d in range(1, PEERS):
        t_copy(d).start()

    for h in range(HEADS):
        g_h = gt[h * COLS : (h + 1) * COLS].reshape(FH, DK)
        m_h = mt[h * COLS : (h + 1) * COLS].reshape(FH, DK)
        both = (tn(g_h, m_h) + tn(m_h, g_h)).astype(BF)
        out_k[:, head(h)] += nn(zz[...], g_h) * (1.0 / SEG) - nn(kk[:, head(h)], both) * (
            rate[0, h] / SEG
        )

    @pl.loop(1, SEGS // 2)
    def _(d):
        r_copy(d).wait()

    out_r[...] = jnp.sum(rall[...].astype(F32), axis=0)

    for d in range(1, PEERS):
        t_copy(d).wait()
    grad = tparts[my].astype(F32)
    for d in range(1, PEERS):
        grad += tparts[PEERS + d].astype(F32)
    out_z[...] = grad


def finish_kernel(*refs):
    half = len(refs) // 2
    for src, dst in zip(refs[:half], refs[half:]):
        dst[...] = src[...]


def shape(dims, kind):
    return jax.ShapeDtypeStruct(dims, kind)


def dma(*dims):
    return pltpu.SemaphoreType.DMA(dims)


def on_device(
    queries, key_rows, value_rows, targets, readout, retain, learn_rate, allowed, positions, grad_out
):
    block = (SEG, WIDE)
    sums = [
        pltpu.VMEM((PEERS, NM, FH // PEERS), F32),
        pltpu.VMEM((PEERS, NM, FH // PEERS), F32),
        pltpu.VMEM((PEERS, NM, FH // PEERS), BF),
    ]
    er_all, mt, k1, v1, k2, v2, q1, g1, q2, g2, hid, tok, picked = pl.pallas_call(
        forward_kernel,
        out_shape=(
            shape((SEGS, DK + ROWS_R, DK), BF),
            shape((SEGS, PIECE, DK), BF),
        )
        + (shape(block, BF),) * 8
        + (
            shape((NM, FH), BF),
            shape((NM, 2 * WIDE), BF),
            shape((NM, WIDE), BF),
        ),
        in_specs=[SM, SM, VM, VM, VM, VM, ANY, ANY, ANY, ANY, VM],
        out_specs=(VM, VM) + (ANY,) * 8 + (VM, VM, VM),
        scratch_shapes=[
            pltpu.VMEM((HEADS, DK + ROWS_R, DK), BF),
            pltpu.VMEM((SEGS, PIECE, DK), BF),
            pltpu.VMEM((SEGS, DK + ROWS_R, DK), BF),
            pltpu.VMEM((SEGS, PIECE, DK), BF),
            pltpu.VMEM((SEGS, PIECE, DK), STATE),
            pltpu.VMEM((SEGS, PIECE, DK), STATE),
        ]
        + sums
        + [
            pltpu.VMEM((PEERS, NM, FH // PEERS), F32),
            pltpu.VMEM((PIECE, DK), F32),
            dma(4), dma(4), dma(SEGS), dma(SEGS), dma(SEGS), dma(SEGS),
            dma(8), dma(8), dma(2 * PEERS), dma(2 * PEERS), dma(8), dma(8), dma(3),
        ],
        compiler_params=pltpu.CompilerParams(
            collective_id=0, has_side_effects=True, vmem_limit_bytes=LIMIT
        ),
        name="forward_scan",
    )(
        retain, learn_rate, queries, key_rows, targets, positions,
        key_rows, value_rows, queries, grad_out, readout,
    )

    segment = lax.axis_index("ctx")
    row = lax.dynamic_slice(allowed, (segment, 0), (1, 2))
    reach = lax.broadcasted_iota(jnp.int32, (1, 2), 1) < segment
    bias = jnp.where((row == 1) & reach, 0.0, NEG).astype(F32)
    results = (
        shape(block, F32),
        shape(block, F32),
        shape(block, F32),
        shape((SEG, FH // PEERS), F32),
        shape((FH // SEGS, 2 * WIDE), F32),
    )
    outs = pl.pallas_call(
        backward_kernel,
        out_shape=results,
        in_specs=[SM, SM] + [VM] * 5 + [ANY] * 15,
        out_specs=(VM,) * 5,
        scratch_shapes=[
            pltpu.VMEM(block, BF),
        ] * 12
        + [
            pltpu.VMEM((SEGS, PIECE, DK), BF),
            pltpu.VMEM((SEGS, DK + ROWS_R, DK), BF),
            pltpu.VMEM(block, BF),
            pltpu.VMEM((NM, 2 * WIDE), BF),
            pltpu.VMEM((8 * HEADS, SEG), F32),
            pltpu.VMEM((HEADS, SEG, 3 * SEG + NM), BF),
            pltpu.VMEM((HEADS, SEG, SEG), BF),
        ]
        + [pltpu.VMEM((PEERS, NM, FH // PEERS), F32)]
        + sums
        + [
            pltpu.VMEM((SEGS, PIECE, DK), BF),
            pltpu.VMEM((SEGS, PIECE, DK), BF),
            pltpu.VMEM((SEGS, PIECE, DK), BF),
            pltpu.VMEM((SEGS, PIECE, DK), BF),
            pltpu.VMEM((2, SEGS // 2, FH // SEGS, 2 * WIDE), F32),
            pltpu.VMEM((2, SEGS // 2, FH // SEGS, 2 * WIDE), BF),
            pltpu.VMEM((SEGS // 2, FH // SEGS, 2 * WIDE), BF),
            pltpu.VMEM((SEGS // 2, FH // SEGS, 2 * WIDE), BF),
            pltpu.VMEM((SEGS // 2, FH // SEGS, 2 * WIDE), BF),
            pltpu.VMEM((2 * PEERS, SEG, FH // PEERS), BF),
            pltpu.VMEM((2, 8 * HEADS, SEG), F32),
            pltpu.VMEM((PIECE, DK), F32),
            dma(SEGS), dma(SEGS), dma(SEGS), dma(SEGS), dma(SEGS // 2), dma(SEGS // 2),
            dma(2 * PEERS), dma(2 * PEERS), dma(PEERS), dma(PEERS), dma(2), dma(2), dma(3), dma(15),
        ],
        compiler_params=pltpu.CompilerParams(
            collective_id=1, has_side_effects=True, vmem_limit_bytes=LIMIT
        ),
        name="backward_scan",
    )(
        learn_rate, bias, tok, readout, picked, hid, positions,
        queries, grad_out, key_rows, value_rows, k1, v1, k2, v2, q1, g1, q2, g2, mt, er_all, targets,
    )
    specs = (
        (pl.BlockSpec((SEG // 4, WIDE), lambda i: (i, 0)),) * 3
        + (pl.BlockSpec((SEG // 4, FH // PEERS), lambda i: (i, 0)),)
        + (pl.BlockSpec((FH // SEGS, 2 * DK), lambda i: (0, i)),)
    )
    return pl.pallas_call(
        finish_kernel, grid=(4,), out_shape=results, in_specs=list(specs), out_specs=specs, name="finish"
    )(*outs)


def solution(mesh):
    return jax.shard_map(
        on_device,
        mesh=mesh,
        in_specs=(
            P("ctx", "head"),
            P("ctx", "head"),
            P("ctx", "head"),
            P("ctx", None),
            P(None, "head"),
            P("ctx", "head"),
            P("ctx", "head"),
            P(),
            P("ctx", None),
            P("ctx", "head"),
        ),
        out_specs=(P("ctx", "head"),) * 5,
        check_vma=False,
    )
```

```python
import functools

import jax
import jax.numpy as jnp
from jax import lax
from jax.experimental import pallas as pl
from jax.experimental.pallas import tpu as pltpu
from jax.sharding import PartitionSpec as P

MESH = pl.DeviceIdType.MESH
BF = jnp.bfloat16
F32 = jnp.float32
NEG = -1e30
STATE = F32
SEGS, HEADS, DK, FH, SEG, NM, PEERS = 32, 4, 128, 512, 512, 128, 4
WIDE = HEADS * DK
COLS = SEGS // HEADS
PIECE = FH // COLS
ROWS_R = 16
VM = pl.BlockSpec(memory_space=pltpu.VMEM)
SM = pl.BlockSpec(memory_space=pltpu.SMEM)
ANY = pl.BlockSpec(memory_space=pl.ANY)
LIMIT = 60 * 1024 * 1024


def nn(a, b):
    return lax.dot_general(a, b, (((1,), (0,)), ((), ())), preferred_element_type=F32)


def nt(a, b):
    return lax.dot_general(a, b, (((1,), (1,)), ((), ())), preferred_element_type=F32)


def tn(a, b):
    return lax.dot_general(a, b, (((0,), (0,)), ((), ())), preferred_element_type=F32)


def head(h):
    return slice(h * DK, (h + 1) * DK)


def local_maps(retain, rate, q, k, z, pos, er, bt, picked):
    onehot = (
        lax.broadcasted_iota(jnp.int32, (SEG, NM), 0) == pos[...]
    ).astype(F32).astype(BF)
    row = lax.broadcasted_iota(jnp.int32, (ROWS_R, DK), 0)
    for h in range(HEADS):
        kh = k[:, head(h)]
        er[h, 0:DK, :] = (tn(kh, kh) * (rate[0, h] / SEG)).astype(BF)
        whole = jnp.full((ROWS_R, DK), retain[0, h], F32)
        first = whole.astype(BF).astype(F32)
        second = (whole - first).astype(BF).astype(F32)
        third = whole - first - second
        er[h, DK:, :] = jnp.where(
            row == 0, first, jnp.where(row == 1, second, jnp.where(row == 2, third, 0.0))
        ).astype(BF)
    for h in range(HEADS):
        bt[h * COLS : (h + 1) * COLS] = (
            (tn(z[...], k[:, head(h)]) * (1.0 / SEG)).astype(BF).reshape(COLS, PIECE, DK)
        )
    picked[...] = tn(onehot, q[...]).astype(BF)


def remote(src, dst, send, recv, where):
    return pltpu.make_async_remote_copy(
        src_ref=src, dst_ref=dst, send_sem=send, recv_sem=recv, device_id=where, device_id_type=MESH
    )


def greet(me, my):
    barrier = pltpu.get_barrier_semaphore()

    @pl.loop(1, SEGS)
    def _(d):
        pl.semaphore_signal(
            barrier, inc=1, device_id={"ctx": lax.rem(me + d, SEGS)}, device_id_type=MESH
        )

    for d in range(1, PEERS):
        pl.semaphore_signal(
            barrier, inc=1, device_id={"head": lax.rem(my + d, PEERS)}, device_id_type=MESH
        )
    return lambda: pl.semaphore_wait(barrier, SEGS - 1 + PEERS - 1)


def place(dev):
    return lax.div(dev, 8), lax.rem(lax.div(dev, 2), 4), lax.rem(dev, 2)


def slot(dev):
    z, x, core = place(dev)
    return x * COLS + z * 2 + core


def er_slot(dev):
    z, x, core = place(dev)
    return core * 16 + z * 4 + x


def step(old, er_all, t, add):
    high = old.astype(BF)
    low = (old - high.astype(F32)).astype(BF)
    e = er_slot(t)
    decay = nn(jnp.concatenate([high, low], axis=0), er_all[e, 0:DK, :])
    share = jnp.sum(er_all[e, DK:, :].astype(F32), axis=0, keepdims=True)
    return share * old - (decay[:PIECE] + decay[PIECE:]) + add.astype(F32)


def sum_over_heads(block, mine, landing, gathered, my, s_y, r_y):
    for d in range(PEERS):
        mine[d] = block(lax.rem(my + d, PEERS))

    def scatter(d):
        to = lax.rem(my + d, PEERS)
        return remote(mine.at[d], landing.at[d], s_y.at[d], r_y.at[d], {"head": to})

    def gather(d):
        to = lax.rem(my + d, PEERS)
        return remote(gathered.at[my], gathered.at[my], s_y.at[PEERS + d], r_y.at[PEERS + d], {"head": to})

    def started():
        for d in range(1, PEERS):
            scatter(d).start()

    def summed():
        total = mine[0]
        for d in range(1, PEERS):
            scatter(d).wait_recv()
            total = total + landing[d]
        gathered[my] = total.astype(BF)
        for d in range(1, PEERS):
            gather(d).start()

    def finished():
        for d in range(1, PEERS):
            src = lax.rem(my + PEERS - d, PEERS)
            remote(
                gathered.at[src], gathered.at[src], s_y.at[PEERS + d], r_y.at[PEERS + d], {"head": src}
            ).wait_recv()
        for d in range(1, PEERS):
            scatter(d).wait_send()
            gather(d).wait_send()
        return jnp.concatenate([gathered[j] for j in range(PEERS)], axis=1)

    return started, summed, finished


def whole_kernel(
    retain, rate, bias, qq, kk, zz, pos, v_h, g_h, readout_h,
    out_q, out_k, out_v, out_z, out_r,
    vv, gg, k1, v1, k2, v2, q1, g1, q2, g2, readout,
    er, bt, picked, hid, tok, er_all, bt_all, outb, landed, mt,
    mine_y, land_y, gath_y, mine_w, land_w, gath_w, part, state,
    gm, stats, scores_grad, own_probs, gsb, gs_all, gout, gt, rterm, rlow, rpair, rbuf, rall, tparts, st_in,
    s_er, r_er, s_bt, r_bt, s_m, r_m, s_halo, r_halo, s_y, r_y, s_z, r_z,
    s_gs, r_gs, s_g, r_g, s_r, r_r, s_w, r_w, s_t, r_t, s_st, r_st, loc, fetch,
):
    me, my = lax.axis_index("ctx"), lax.axis_index("head")
    mz, mx, core = place(me)
    partner = me + 1 - 2 * core
    scale = DK**-0.5
    entered = greet(me, my)
    fetched = [
        pltpu.make_async_copy(src, dst, fetch.at[i])
        for i, (src, dst) in enumerate(((v_h, vv), (g_h, gg), (readout_h, readout)))
    ]
    for copy in fetched:
        copy.start()
    local_maps(retain, rate, qq, kk, zz, pos, er, bt, picked)
    entered()

    def er_copy(x, to_x):
        return remote(
            er.at[to_x], er_all.at[core * 16 + mz * 4 + x], s_er.at[to_x], r_er.at[x],
            {"ctx": mz * 8 + to_x * 2 + core},
        )

    def block(side, z):
        return er_all.at[pl.ds(side * 16 + z * 4, 4)]

    def over_z(d):
        to = lax.rem(mz + d, 4)
        return remote(
            block(core, mz), block(core, mz), s_z.at[d], r_z.at[d], {"ctx": to * 8 + mx * 2 + core}
        )

    def over_core(d, side):
        z = lax.rem(mz + 4 - d, 4)
        return remote(block(side, z), block(side, z), s_z.at[4 + d], r_z.at[4 + d], {"ctx": partner})

    def bt_copy(to, src):
        return remote(bt.at[slot(to)], bt_all.at[src], s_bt.at[to], r_bt.at[src], {"ctx": to})

    def m_copy(to, src):
        return remote(outb.at[to], landed.at[slot(src)], s_m.at[to], r_m.at[src], {"ctx": to})

    for d in range(1, 4):
        er_copy(mx, lax.rem(mx + d, 4)).start()
    own_er = pltpu.make_async_copy(er.at[mx], er_all.at[er_slot(me)], loc.at[0])
    own_bt = pltpu.make_async_copy(bt.at[slot(me)], bt_all.at[me], loc.at[1])
    own_er.start()
    own_bt.start()

    @pl.loop(1, SEGS)
    def _(d):
        bt_copy(lax.rem(me + d, SEGS), me).start()

    def halo(src, dst, i, to):
        return remote(src, dst, s_halo.at[i], r_halo.at[i], {"ctx": to})

    after, before = lax.rem(me + 2, SEGS), lax.rem(me + SEGS - 2, SEGS)
    far = [
        halo(vv, v2, 0, after),
        halo(gg, g2, 1, before),
        halo(kk, k2, 2, after),
        halo(qq, q2, 3, before),
    ]
    keys_near = [halo(vv, v1, 4, partner), halo(kk, k1, 6, partner)]
    rows_near = [halo(gg, g1, 5, partner), halo(qq, q1, 7, partner)]
    keys_relay = [halo(v2, v1, 4, partner), halo(k2, k1, 6, partner)]
    rows_relay = [halo(g2, g1, 5, partner), halo(q2, q1, 7, partner)]

    def relay(i):
        far[2 * i].wait_recv()
        far[2 * i + 1].wait_recv()

        @pl.when(core == 1)
        def _():
            keys_relay[i].start()

        @pl.when(core == 0)
        def _():
            rows_relay[i].start()

    own_er.wait()
    own_bt.wait()
    for d in range(1, 4):
        er_copy(lax.rem(mx + 4 - d, 4), mx).wait_recv()
    for d in range(1, 4):
        over_z(d).start()
    over_core(0, core).start()
    for d in range(1, 4):
        over_z(d).wait_recv()
        over_core(d, core).start()

    @pl.loop(1, SEGS)
    def _(d):
        bt_copy(lax.rem(me + d, SEGS), me).wait_send()

    for copy in fetched:
        copy.wait()
    for copy in far[:2]:
        copy.start()

    @pl.when(core == 0)
    def _():
        for copy in keys_near:
            copy.start()

    @pl.when(core == 1)
    def _():
        for copy in rows_near:
            copy.start()

    @pl.loop(1, SEGS)
    def _(d):
        src = lax.rem(me + SEGS - d, SEGS)
        bt_copy(src, src).wait_recv()

    for d in range(4):
        over_core(d, 1 - core).wait_recv()

    state[...] = jnp.zeros((PIECE, DK), F32)

    @pl.loop(0, SEGS)
    def _(t):
        old = state[...]
        outb[t] = old.astype(outb.dtype)
        state[...] = step(old, er_all, t, bt_all[t])

    @pl.loop(1, SEGS)
    def _(d):
        m_copy(lax.rem(me + d, SEGS), me).start()

    own_m = pltpu.make_async_copy(outb.at[me], landed.at[slot(me)], loc.at[2])
    own_m.start()
    own_m.wait()

    @pl.loop(1, SEGS)
    def _(d):
        m_copy(lax.rem(me + d, SEGS), me).wait_send()

    for copy in far[2:]:
        copy.start()

    @pl.loop(1, SEGS)
    def _(d):
        src = lax.rem(me + d, SEGS)
        m_copy(src, src).wait_recv()

    for h in range(HEADS):
        m_h = landed[h * COLS : (h + 1) * COLS].reshape(FH, DK)
        high = m_h.astype(BF)
        mt[h * COLS : (h + 1) * COLS] = high.reshape(COLS, PIECE, DK)
        term = nt(picked[:, head(h)], high)
        if STATE == F32:
            term += nt(picked[:, head(h)], (m_h - high.astype(F32)).astype(BF))
        for j in range(PEERS):
            if h == 0:
                part[j] = term[:, head(j)]
            else:
                part[j] += term[:, head(j)]
    started, summed, finished = sum_over_heads(lambda j: part[j], mine_y, land_y, gath_y, my, s_y, r_y)
    started()
    relay(0)
    summed()
    relay(1)
    low = finished()
    hid[...] = low
    tok[...] = nn(low, readout[...]).astype(BF)
    for copy in keys_near:
        copy.wait_recv()

    @pl.loop(0, HEADS)
    def _(h):
        lanes = pl.ds(pl.multiple_of(h * DK, DK), DK)
        tok_k = pl.ds(pl.multiple_of(h * 2 * DK, DK), DK)
        tok_v = pl.ds(pl.multiple_of(h * 2 * DK + DK, DK), DK)
        q_t, g_t = qq[:, lanes], gg[:, lanes]
        causal = lax.broadcasted_iota(jnp.int32, (SEG, SEG), 0) >= lax.broadcasted_iota(
            jnp.int32, (SEG, SEG), 1
        )
        keys = [kk[:, lanes], k1[:, lanes], k2[:, lanes], tok[:, tok_k]]
        vals = [vv[:, lanes], v1[:, lanes], v2[:, lanes], tok[:, tok_v]]
        scores = [nt(q_t, key) for key in keys]
        scores[0] = jnp.where(causal, scores[0], NEG)
        scores[1] = scores[1] + bias[0, 0]
        scores[2] = scores[2] + bias[0, 1]
        top = functools.reduce(jnp.maximum, [jnp.max(s, axis=1, keepdims=True) for s in scores])
        exps = [jnp.exp((s - top) * scale) for s in scores]
        total = functools.reduce(jnp.add, [jnp.sum(e, axis=1, keepdims=True) for e in exps])
        inverse = 1.0 / total
        probs = [e * inverse for e in exps]
        lows = [p.astype(BF) for p in probs]
        attended = functools.reduce(jnp.add, [nn(p, value) for p, value in zip(lows, vals)])
        delta = jnp.sum(g_t.astype(F32) * attended, axis=1, keepdims=True)
        grads = [
            (p * (nt(g_t, value) - delta)).astype(BF) for p, value in zip(probs, vals)
        ]
        gm[:, tok_k] = (tn(grads[3], q_t) * scale).astype(BF)
        gm[:, tok_v] = tn(lows[3], g_t).astype(BF)
        own_probs[h] = lows[0]
        for i in range(3):
            scores_grad[h, :, i * SEG : (i + 1) * SEG] = grads[i]
        scores_grad[h, :, 3 * SEG :] = grads[3]
        level = top * scale + jnp.log(total)
        lane = lax.broadcasted_iota(jnp.int32, (SEG, DK), 1)
        columns = jnp.where(
            lane == 0, level - bias[0, 0], jnp.where(lane == 1, level - bias[0, 1], delta)
        )
        stats[pl.ds(pl.multiple_of(h * 8, 8), 8), :] = columns.T[0:8, :]

    def stat_copy(o):
        to = lax.rem(me + SEGS - o, SEGS)
        return remote(stats, st_in.at[o - 1], s_st.at[o - 1], r_st.at[o - 1], {"ctx": to})

    def gs_copy(to, src):
        return remote(gsb.at[slot(to)], gs_all.at[src], s_gs.at[to], r_gs.at[src], {"ctx": to})

    def g_copy(to, src):
        return remote(gout.at[to], gt.at[slot(src)], s_g.at[to], r_g.at[src], {"ctx": to})

    chip = lax.div(me, 2)
    pair = remote(rlow.at[1 - core], rpair, s_r.at[0], r_r.at[0], {"ctx": partner})

    def r_copy(d):
        to = lax.rem(chip + d, SEGS // 2)
        return remote(rbuf.at[to], rall.at[chip], s_r.at[d], r_r.at[d], {"ctx": to * 2 + core})

    def own_tile(h):
        grad = scores_grad[h, :, 0:SEG]
        out_q[:, head(h)] = (
            nn(grad, kk[:, head(h)])
            + nn(scores_grad[h, :, SEG : 2 * SEG], k1[:, head(h)])
            + nn(scores_grad[h, :, 2 * SEG : 3 * SEG], k2[:, head(h)])
            + nn(scores_grad[h, :, 3 * SEG :], tok[:, 2 * h * DK : (2 * h + 1) * DK])
        ) * scale
        out_k[:, head(h)] = tn(grad, qq[:, head(h)]) * scale
        out_v[:, head(h)] = tn(own_probs[h], gg[:, head(h)])

    def far_tile(o, h):
        q_t, g_t = (q1, g1) if o == 1 else (q2, g2)
        q_t, g_t = q_t[:, head(h)], g_t[:, head(h)]
        level = st_in[o - 1, 8 * h + o - 1 : 8 * h + o, :]
        delta = st_in[o - 1, 8 * h + 2 : 8 * h + 3, :]
        probs = jnp.exp(nt(kk[:, head(h)], q_t) * scale - level)
        grads = probs * (nt(vv[:, head(h)], g_t) - delta)
        out_v[:, head(h)] += nn(probs.astype(BF), g_t)
        out_k[:, head(h)] += nn(grads.astype(BF), q_t) * scale

    term = nt(gm[...], readout[...])
    for j in range(PEERS):
        part[j] = term[:, head(j)]
    started, summed, finished = sum_over_heads(lambda j: part[j], mine_w, land_w, gath_w, my, s_w, r_w)
    started()
    for o in (1, 2):
        stat_copy(o).start()
    term = tn(hid[...], gm[...]).reshape(SEGS // 2, 2, FH // SEGS, 2 * WIDE)
    for side in range(2):
        rterm[side] = term[:, side]
        rlow[side] = term[:, side].astype(BF)
    pair.start()
    own_tile(0)
    own_tile(1)
    summed()
    own_tile(2)
    own_tile(3)
    gh = finished()

    for h in range(HEADS):
        gsb[h * COLS : (h + 1) * COLS] = (
            tn(gh, picked[:, head(h)]).astype(BF).reshape(COLS, PIECE, DK)
        )

    @pl.loop(1, SEGS)
    def _(d):
        gs_copy(lax.rem(me + d, SEGS), me).start()

    own_gs = pltpu.make_async_copy(gsb.at[slot(me)], gs_all.at[me], loc.at[3])
    own_gs.start()
    for o in (1, 2):
        stat_copy(o).wait()
    for copy in rows_near:
        copy.wait_recv()
    far_tile(1, 0)
    far_tile(2, 0)
    pair.wait()
    rbuf[...] = (rterm[core] + rpair[...].astype(F32)).astype(BF)
    far_tile(1, 1)

    @pl.loop(1, SEGS // 2)
    def _(d):
        r_copy(d).start()

    own_r = pltpu.make_async_copy(rbuf.at[chip], rall.at[chip], loc.at[4])
    own_r.start()
    far_tile(2, 1)
    far_tile(1, 2)
    far_tile(2, 2)

    own_gs.wait()
    own_r.wait()

    @pl.loop(1, SEGS)
    def _(d):
        src = lax.rem(me + SEGS - d, SEGS)
        gs_copy(src, src).wait_recv()

    state[...] = jnp.zeros((PIECE, DK), F32)

    @pl.loop(0, SEGS)
    def _(i):
        t = SEGS - 1 - i
        old = state[...]
        gout[t] = old.astype(BF)
        state[...] = step(old, er_all, t, gs_all[t])

    @pl.loop(1, SEGS)
    def _(d):
        g_copy(lax.rem(me + d, SEGS), me).start()

    own_g = pltpu.make_async_copy(gout.at[me], gt.at[slot(me)], loc.at[5])
    own_g.start()
    far_tile(1, 3)
    far_tile(2, 3)

    onehot = (
        lax.broadcasted_iota(jnp.int32, (SEG, NM), 0) == pos[...]
    ).astype(F32).astype(BF)
    for h in range(HEADS):
        m_h = mt[h * COLS : (h + 1) * COLS].reshape(FH, DK)
        grad_picked = nn(gh, m_h).astype(BF)
        out_q[:, head(h)] += nn(onehot, grad_picked)

    own_g.wait()

    @pl.loop(1, SEGS)
    def _(d):
        to = lax.rem(me + d, SEGS)
        gs_copy(to, me).wait_send()
        g_copy(to, me).wait_send()
        g_copy(to, to).wait_recv()

    term = jnp.zeros((SEG, FH), F32)
    for h in range(HEADS):
        g_h = gt[h * COLS : (h + 1) * COLS].reshape(FH, DK)
        term += nt(kk[:, head(h)], g_h)
    term = (term * (1.0 / SEG)).astype(BF)
    for j in range(PEERS):
        tparts[j] = term[:, head(j)]

    def t_copy(d):
        to = lax.rem(my + d, PEERS)
        return remote(tparts.at[to], tparts.at[PEERS + d], s_t.at[d], r_t.at[d], {"head": to})

    for d in range(1, PEERS):
        t_copy(d).start()

    for h in range(HEADS):
        g_h = gt[h * COLS : (h + 1) * COLS].reshape(FH, DK)
        m_h = mt[h * COLS : (h + 1) * COLS].reshape(FH, DK)
        both = (tn(g_h, m_h) + tn(m_h, g_h)).astype(BF)
        out_k[:, head(h)] += nn(zz[...], g_h) * (1.0 / SEG) - nn(kk[:, head(h)], both) * (
            rate[0, h] / SEG
        )

    @pl.loop(1, SEGS // 2)
    def _(d):
        r_copy(d).wait()

    out_r[...] = jnp.sum(rall[...].astype(F32), axis=0)

    for d in range(1, PEERS):
        t_copy(d).wait()
    grad = tparts[my].astype(F32)
    for d in range(1, PEERS):
        grad += tparts[PEERS + d].astype(F32)
    out_z[...] = grad
    for d in range(1, 4):
        er_copy(mx, lax.rem(mx + d, 4)).wait_send()
        over_z(d).wait_send()
    for d in range(4):
        over_core(d, core).wait_send()
    for copy in far + keys_near + rows_near:
        copy.wait_send()


def finish_kernel(*refs):
    count = len(refs) // 3
    arrays, (load, store) = refs[: 2 * count], refs[3 * count :]
    held = refs[2 * count : 3 * count]
    loads, stores = [], []
    for i in range(count):
        half = arrays[i].shape[0] // 2
        for part in range(2):
            rows = pl.ds(part * half, half)
            slot_of = 2 * i + part
            loads.append(pltpu.make_async_copy(arrays[i].at[rows], held[i].at[rows], load.at[slot_of]))
            stores.append(
                pltpu.make_async_copy(held[i].at[rows], arrays[count + i].at[rows], store.at[slot_of])
            )
    for copy in loads:
        copy.start()
    for first, then in zip(loads, stores):
        first.wait()
        then.start()
    for copy in stores:
        copy.wait()


def shape(dims, kind):
    return jax.ShapeDtypeStruct(dims, kind)


def dma(*dims):
    return pltpu.SemaphoreType.DMA(dims)


def on_device(
    queries, key_rows, value_rows, targets, readout, retain, learn_rate, allowed, positions, grad_out
):
    block = (SEG, WIDE)
    segment = lax.axis_index("ctx")
    row = lax.dynamic_slice(allowed, (segment, 0), (1, 2))
    reach = lax.broadcasted_iota(jnp.int32, (1, 2), 1) < segment
    bias = jnp.where((row == 1) & reach, 0.0, NEG).astype(F32)
    results = (
        shape(block, F32),
        shape(block, F32),
        shape(block, F32),
        shape((SEG, FH // PEERS), F32),
        shape((FH // SEGS, 2 * WIDE), F32),
    )
    sums = [
        pltpu.VMEM((PEERS, NM, FH // PEERS), F32),
        pltpu.VMEM((PEERS, NM, FH // PEERS), F32),
        pltpu.VMEM((PEERS, NM, FH // PEERS), BF),
    ]
    low_pieces = pltpu.VMEM((SEGS, PIECE, DK), BF)
    terms = (SEGS // 2, FH // SEGS, 2 * WIDE)
    outs = pl.pallas_call(
        whole_kernel,
        out_shape=results,
        in_specs=[SM, SM, SM] + [VM] * 4 + [ANY] * 3,
        out_specs=(VM,) * 5,
        scratch_shapes=[pltpu.VMEM(block, BF)] * 10
        + [
            pltpu.VMEM((FH, 2 * WIDE), BF),
            pltpu.VMEM((HEADS, DK + ROWS_R, DK), BF),
            low_pieces,
            pltpu.VMEM((NM, WIDE), BF),
            pltpu.VMEM((NM, FH), BF),
            pltpu.VMEM((NM, 2 * WIDE), BF),
            pltpu.VMEM((SEGS, DK + ROWS_R, DK), BF),
            low_pieces,
            pltpu.VMEM((SEGS, PIECE, DK), STATE),
            pltpu.VMEM((SEGS, PIECE, DK), STATE),
            low_pieces,
        ]
        + sums
        + sums
        + [
            pltpu.VMEM((PEERS, NM, FH // PEERS), F32),
            pltpu.VMEM((PIECE, DK), F32),
            pltpu.VMEM((NM, 2 * WIDE), BF),
            pltpu.VMEM((8 * HEADS, SEG), F32),
            pltpu.VMEM((HEADS, SEG, 3 * SEG + NM), BF),
            pltpu.VMEM((HEADS, SEG, SEG), BF),
            low_pieces,
            low_pieces,
            low_pieces,
            low_pieces,
            pltpu.VMEM((2,) + terms, F32),
            pltpu.VMEM((2,) + terms, BF),
            pltpu.VMEM(terms, BF),
            pltpu.VMEM(terms, BF),
            pltpu.VMEM(terms, BF),
            pltpu.VMEM((2 * PEERS, SEG, FH // PEERS), BF),
            pltpu.VMEM((2, 8 * HEADS, SEG), F32),
            dma(4), dma(4), dma(SEGS), dma(SEGS), dma(SEGS), dma(SEGS),
            dma(8), dma(8), dma(2 * PEERS), dma(2 * PEERS), dma(8), dma(8),
            dma(SEGS), dma(SEGS), dma(SEGS), dma(SEGS), dma(SEGS // 2), dma(SEGS // 2),
            dma(2 * PEERS), dma(2 * PEERS), dma(PEERS), dma(PEERS), dma(2), dma(2), dma(6), dma(3),
        ],
        compiler_params=pltpu.CompilerParams(
            collective_id=0, has_side_effects=True, vmem_limit_bytes=LIMIT
        ),
        name="whole",
    )(
        retain, learn_rate, bias, queries, key_rows, targets, positions, value_rows, grad_out, readout,
    )
    return pl.pallas_call(
        finish_kernel,
        out_shape=results,
        in_specs=[ANY] * 5,
        out_specs=(ANY,) * 5,
        scratch_shapes=[pltpu.VMEM(out.shape, F32) for out in results] + [dma(10), dma(10)],
        compiler_params=pltpu.CompilerParams(vmem_limit_bytes=LIMIT),
        name="finish",
    )(*outs)


def solution(mesh):
    return jax.shard_map(
        on_device,
        mesh=mesh,
        in_specs=(
            P("ctx", "head"),
            P("ctx", "head"),
            P("ctx", "head"),
            P("ctx", None),
            P(None, "head"),
            P("ctx", "head"),
            P("ctx", "head"),
            P(),
            P("ctx", None),
            P("ctx", "head"),
        ),
        out_specs=(P("ctx", "head"),) * 5,
        check_vma=False,
    )
```

```python
import functools

import jax
import jax.numpy as jnp
from jax import lax
from jax.experimental import pallas as pl
from jax.experimental.pallas import tpu as pltpu
from jax.sharding import PartitionSpec as P

MESH = pl.DeviceIdType.MESH
BF = jnp.bfloat16
F32 = jnp.float32
NEG = -1e30
STATE = F32
SEGS, HEADS, DK, FH, SEG, NM, PEERS = 32, 4, 128, 512, 512, 128, 4
WIDE = HEADS * DK
COLS = SEGS // HEADS
PIECE = FH // COLS
ROWS_R = 16
VM = pl.BlockSpec(memory_space=pltpu.VMEM)
SM = pl.BlockSpec(memory_space=pltpu.SMEM)
ANY = pl.BlockSpec(memory_space=pl.ANY)
LIMIT = 60 * 1024 * 1024


def nn(a, b):
    return lax.dot_general(a, b, (((1,), (0,)), ((), ())), preferred_element_type=F32)


def nt(a, b):
    return lax.dot_general(a, b, (((1,), (1,)), ((), ())), preferred_element_type=F32)


def tn(a, b):
    return lax.dot_general(a, b, (((0,), (0,)), ((), ())), preferred_element_type=F32)


def head(h):
    return slice(h * DK, (h + 1) * DK)


def local_maps(retain, rate, q, k, z, pos, er, bt, picked):
    onehot = (
        lax.broadcasted_iota(jnp.int32, (SEG, NM), 0) == pos[...]
    ).astype(F32).astype(BF)
    row = lax.broadcasted_iota(jnp.int32, (ROWS_R, DK), 0)
    for h in range(HEADS):
        kh = k[:, head(h)]
        er[h, 0:DK, :] = (tn(kh, kh) * (rate[0, h] / SEG)).astype(BF)
        whole = jnp.full((ROWS_R, DK), retain[0, h], F32)
        first = whole.astype(BF).astype(F32)
        second = (whole - first).astype(BF).astype(F32)
        third = whole - first - second
        er[h, DK:, :] = jnp.where(
            row == 0, first, jnp.where(row == 1, second, jnp.where(row == 2, third, 0.0))
        ).astype(BF)
    for h in range(HEADS):
        bt[h * COLS : (h + 1) * COLS] = (
            (tn(z[...], k[:, head(h)]) * (1.0 / SEG)).astype(BF).reshape(COLS, PIECE, DK)
        )
    picked[...] = tn(onehot, q[...]).astype(BF)


def remote(src, dst, send, recv, where):
    return pltpu.make_async_remote_copy(
        src_ref=src, dst_ref=dst, send_sem=send, recv_sem=recv, device_id=where, device_id_type=MESH
    )


def greet(me, my):
    barrier = pltpu.get_barrier_semaphore()

    @pl.loop(1, SEGS)
    def _(d):
        pl.semaphore_signal(
            barrier, inc=1, device_id={"ctx": lax.rem(me + d, SEGS)}, device_id_type=MESH
        )

    for d in range(1, PEERS):
        pl.semaphore_signal(
            barrier, inc=1, device_id={"head": lax.rem(my + d, PEERS)}, device_id_type=MESH
        )
    return lambda: pl.semaphore_wait(barrier, SEGS - 1 + PEERS - 1)


def place(dev):
    return lax.div(dev, 8), lax.rem(lax.div(dev, 2), 4), lax.rem(dev, 2)


def slot(dev):
    z, x, core = place(dev)
    return x * COLS + z * 2 + core


def er_slot(dev):
    z, x, core = place(dev)
    return core * 16 + z * 4 + x


def step(old, er_all, t, add):
    high = old.astype(BF)
    low = (old - high.astype(F32)).astype(BF)
    e = er_slot(t)
    decay = nn(jnp.concatenate([high, low], axis=0), er_all[e, 0:DK, :])
    share = jnp.sum(er_all[e, DK:, :].astype(F32), axis=0, keepdims=True)
    return share * old - (decay[:PIECE] + decay[PIECE:]) + add.astype(F32)


def sum_over_heads(block, mine, landing, gathered, my, s_y, r_y):
    for d in range(PEERS):
        mine[d] = block(lax.rem(my + d, PEERS))

    def scatter(d):
        to = lax.rem(my + d, PEERS)
        return remote(mine.at[d], landing.at[d], s_y.at[d], r_y.at[d], {"head": to})

    def gather(d):
        to = lax.rem(my + d, PEERS)
        return remote(gathered.at[my], gathered.at[my], s_y.at[PEERS + d], r_y.at[PEERS + d], {"head": to})

    def started():
        for d in range(1, PEERS):
            scatter(d).start()

    def summed():
        total = mine[0]
        for d in range(1, PEERS):
            scatter(d).wait_recv()
            total = total + landing[d]
        gathered[my] = total.astype(BF)
        for d in range(1, PEERS):
            gather(d).start()

    def finished():
        for d in range(1, PEERS):
            src = lax.rem(my + PEERS - d, PEERS)
            remote(
                gathered.at[src], gathered.at[src], s_y.at[PEERS + d], r_y.at[PEERS + d], {"head": src}
            ).wait_recv()
        for d in range(1, PEERS):
            scatter(d).wait_send()
            gather(d).wait_send()
        return jnp.concatenate([gathered[j] for j in range(PEERS)], axis=1)

    return started, summed, finished


def whole_kernel(
    retain, rate, bias, qq, kk, zz, pos, v_h, g_h, readout_h,
    ship_q, out_k, ship_v, out_z, out_r,
    out_q, out_v, vv, gg, k1, v1, k2, v2, q1, g1, q2, g2, readout,
    er, bt, picked, hid, tok, er_all, bt_all, outb, landed, mt,
    mine_y, land_y, gath_y, mine_w, land_w, gath_w, part, state,
    gm, stats, scores_grad, own_probs, gsb, gs_all, gout, gt, rterm, rlow, rpair, rbuf, rall, tparts, st_in,
    s_er, r_er, s_bt, r_bt, s_m, r_m, s_halo, r_halo, s_y, r_y, s_z, r_z,
    s_gs, r_gs, s_g, r_g, s_r, r_r, s_w, r_w, s_t, r_t, s_st, r_st, loc, fetch, ship,
):
    me, my = lax.axis_index("ctx"), lax.axis_index("head")
    mz, mx, core = place(me)
    partner = me + 1 - 2 * core
    scale = DK**-0.5
    entered = greet(me, my)
    fetched = [
        pltpu.make_async_copy(src, dst, fetch.at[i])
        for i, (src, dst) in enumerate(((v_h, vv), (g_h, gg), (readout_h, readout)))
    ]
    for copy in fetched:
        copy.start()
    local_maps(retain, rate, qq, kk, zz, pos, er, bt, picked)
    entered()

    def er_copy(x, to_x):
        return remote(
            er.at[to_x], er_all.at[core * 16 + mz * 4 + x], s_er.at[to_x], r_er.at[x],
            {"ctx": mz * 8 + to_x * 2 + core},
        )

    def block(side, z):
        return er_all.at[pl.ds(side * 16 + z * 4, 4)]

    def over_z(d):
        to = lax.rem(mz + d, 4)
        return remote(
            block(core, mz), block(core, mz), s_z.at[d], r_z.at[d], {"ctx": to * 8 + mx * 2 + core}
        )

    def over_core(d, side):
        z = lax.rem(mz + 4 - d, 4)
        return remote(block(side, z), block(side, z), s_z.at[4 + d], r_z.at[4 + d], {"ctx": partner})

    def bt_copy(to, src):
        return remote(bt.at[slot(to)], bt_all.at[src], s_bt.at[to], r_bt.at[src], {"ctx": to})

    def m_copy(to, src):
        return remote(outb.at[to], landed.at[slot(src)], s_m.at[to], r_m.at[src], {"ctx": to})

    for d in range(1, 4):
        er_copy(mx, lax.rem(mx + d, 4)).start()
    own_er = pltpu.make_async_copy(er.at[mx], er_all.at[er_slot(me)], loc.at[0])
    own_bt = pltpu.make_async_copy(bt.at[slot(me)], bt_all.at[me], loc.at[1])
    own_er.start()
    own_bt.start()

    @pl.loop(1, SEGS)
    def _(d):
        bt_copy(lax.rem(me + d, SEGS), me).start()

    def halo(src, dst, i, to):
        return remote(src, dst, s_halo.at[i], r_halo.at[i], {"ctx": to})

    after, before = lax.rem(me + 2, SEGS), lax.rem(me + SEGS - 2, SEGS)
    far = [
        halo(vv, v2, 0, after),
        halo(gg, g2, 1, before),
        halo(kk, k2, 2, after),
        halo(qq, q2, 3, before),
    ]
    keys_near = [halo(vv, v1, 4, partner), halo(kk, k1, 6, partner)]
    rows_near = [halo(gg, g1, 5, partner), halo(qq, q1, 7, partner)]
    keys_relay = [halo(v2, v1, 4, partner), halo(k2, k1, 6, partner)]
    rows_relay = [halo(g2, g1, 5, partner), halo(q2, q1, 7, partner)]

    def relay(i):
        far[2 * i].wait_recv()
        far[2 * i + 1].wait_recv()

        @pl.when(core == 1)
        def _():
            keys_relay[i].start()

        @pl.when(core == 0)
        def _():
            rows_relay[i].start()

    own_er.wait()
    own_bt.wait()
    for d in range(1, 4):
        er_copy(lax.rem(mx + 4 - d, 4), mx).wait_recv()
    for d in range(1, 4):
        over_z(d).start()
    over_core(0, core).start()
    for d in range(1, 4):
        over_z(d).wait_recv()
        over_core(d, core).start()

    @pl.loop(1, SEGS)
    def _(d):
        bt_copy(lax.rem(me + d, SEGS), me).wait_send()

    for copy in fetched:
        copy.wait()
    for copy in far[:2]:
        copy.start()

    @pl.when(core == 0)
    def _():
        for copy in keys_near:
            copy.start()

    @pl.when(core == 1)
    def _():
        for copy in rows_near:
            copy.start()

    @pl.loop(1, SEGS)
    def _(d):
        src = lax.rem(me + SEGS - d, SEGS)
        bt_copy(src, src).wait_recv()

    for d in range(4):
        over_core(d, 1 - core).wait_recv()

    state[...] = jnp.zeros((PIECE, DK), F32)

    @pl.loop(0, SEGS)
    def _(t):
        old = state[...]
        outb[t] = old.astype(outb.dtype)
        state[...] = step(old, er_all, t, bt_all[t])

    @pl.loop(1, SEGS)
    def _(d):
        m_copy(lax.rem(me + d, SEGS), me).start()

    own_m = pltpu.make_async_copy(outb.at[me], landed.at[slot(me)], loc.at[2])
    own_m.start()
    own_m.wait()

    @pl.loop(1, SEGS)
    def _(d):
        m_copy(lax.rem(me + d, SEGS), me).wait_send()

    for copy in far[2:]:
        copy.start()

    @pl.loop(1, SEGS)
    def _(d):
        src = lax.rem(me + d, SEGS)
        m_copy(src, src).wait_recv()

    for h in range(HEADS):
        m_h = landed[h * COLS : (h + 1) * COLS].reshape(FH, DK)
        high = m_h.astype(BF)
        mt[h * COLS : (h + 1) * COLS] = high.reshape(COLS, PIECE, DK)
        term = nt(picked[:, head(h)], high)
        if STATE == F32:
            term += nt(picked[:, head(h)], (m_h - high.astype(F32)).astype(BF))
        for j in range(PEERS):
            if h == 0:
                part[j] = term[:, head(j)]
            else:
                part[j] += term[:, head(j)]
    started, summed, finished = sum_over_heads(lambda j: part[j], mine_y, land_y, gath_y, my, s_y, r_y)
    started()
    relay(0)
    summed()
    relay(1)
    low = finished()
    hid[...] = low
    tok[...] = nn(low, readout[...]).astype(BF)
    for copy in keys_near:
        copy.wait_recv()

    @pl.loop(0, HEADS)
    def _(h):
        lanes = pl.ds(pl.multiple_of(h * DK, DK), DK)
        tok_k = pl.ds(pl.multiple_of(h * 2 * DK, DK), DK)
        tok_v = pl.ds(pl.multiple_of(h * 2 * DK + DK, DK), DK)
        q_t, g_t = qq[:, lanes], gg[:, lanes]
        causal = lax.broadcasted_iota(jnp.int32, (SEG, SEG), 0) >= lax.broadcasted_iota(
            jnp.int32, (SEG, SEG), 1
        )
        keys = [kk[:, lanes], k1[:, lanes], k2[:, lanes], tok[:, tok_k]]
        vals = [vv[:, lanes], v1[:, lanes], v2[:, lanes], tok[:, tok_v]]
        scores = [nt(q_t, key) for key in keys]
        scores[0] = jnp.where(causal, scores[0], NEG)
        scores[1] = scores[1] + bias[0, 0]
        scores[2] = scores[2] + bias[0, 1]
        top = functools.reduce(jnp.maximum, [jnp.max(s, axis=1, keepdims=True) for s in scores])
        exps = [jnp.exp((s - top) * scale) for s in scores]
        total = functools.reduce(jnp.add, [jnp.sum(e, axis=1, keepdims=True) for e in exps])
        inverse = 1.0 / total
        probs = [e * inverse for e in exps]
        lows = [p.astype(BF) for p in probs]
        attended = functools.reduce(jnp.add, [nn(p, value) for p, value in zip(lows, vals)])
        delta = jnp.sum(g_t.astype(F32) * attended, axis=1, keepdims=True)
        grads = [
            (p * (nt(g_t, value) - delta)).astype(BF) for p, value in zip(probs, vals)
        ]
        gm[:, tok_k] = (tn(grads[3], q_t) * scale).astype(BF)
        gm[:, tok_v] = tn(lows[3], g_t).astype(BF)
        own_probs[h] = lows[0]
        for i in range(3):
            scores_grad[h, :, i * SEG : (i + 1) * SEG] = grads[i]
        scores_grad[h, :, 3 * SEG :] = grads[3]
        level = top * scale + jnp.log(total)
        lane = lax.broadcasted_iota(jnp.int32, (SEG, DK), 1)
        columns = jnp.where(
            lane == 0, level - bias[0, 0], jnp.where(lane == 1, level - bias[0, 1], delta)
        )
        stats[pl.ds(pl.multiple_of(h * 8, 8), 8), :] = columns.T[0:8, :]

    def stat_copy(o):
        to = lax.rem(me + SEGS - o, SEGS)
        return remote(stats, st_in.at[o - 1], s_st.at[o - 1], r_st.at[o - 1], {"ctx": to})

    def gs_copy(to, src):
        return remote(gsb.at[slot(to)], gs_all.at[src], s_gs.at[to], r_gs.at[src], {"ctx": to})

    def g_copy(to, src):
        return remote(gout.at[to], gt.at[slot(src)], s_g.at[to], r_g.at[src], {"ctx": to})

    chip = lax.div(me, 2)
    pair = remote(rlow.at[1 - core], rpair, s_r.at[0], r_r.at[0], {"ctx": partner})

    def r_copy(d):
        to = lax.rem(chip + d, SEGS // 2)
        return remote(rbuf.at[to], rall.at[chip], s_r.at[d], r_r.at[d], {"ctx": to * 2 + core})

    def own_tile(h):
        grad = scores_grad[h, :, 0:SEG]
        out_q[:, head(h)] = (
            nn(grad, kk[:, head(h)])
            + nn(scores_grad[h, :, SEG : 2 * SEG], k1[:, head(h)])
            + nn(scores_grad[h, :, 2 * SEG : 3 * SEG], k2[:, head(h)])
            + nn(scores_grad[h, :, 3 * SEG :], tok[:, 2 * h * DK : (2 * h + 1) * DK])
        ) * scale
        out_k[:, head(h)] = tn(grad, qq[:, head(h)]) * scale
        out_v[:, head(h)] = tn(own_probs[h], gg[:, head(h)])

    def far_tile(o, h):
        q_t, g_t = (q1, g1) if o == 1 else (q2, g2)
        q_t, g_t = q_t[:, head(h)], g_t[:, head(h)]
        level = st_in[o - 1, 8 * h + o - 1 : 8 * h + o, :]
        delta = st_in[o - 1, 8 * h + 2 : 8 * h + 3, :]
        probs = jnp.exp(nt(kk[:, head(h)], q_t) * scale - level)
        grads = probs * (nt(vv[:, head(h)], g_t) - delta)
        out_v[:, head(h)] += nn(probs.astype(BF), g_t)
        out_k[:, head(h)] += nn(grads.astype(BF), q_t) * scale

    term = nt(gm[...], readout[...])
    for j in range(PEERS):
        part[j] = term[:, head(j)]
    started, summed, finished = sum_over_heads(lambda j: part[j], mine_w, land_w, gath_w, my, s_w, r_w)
    started()
    for o in (1, 2):
        stat_copy(o).start()
    term = tn(hid[...], gm[...]).reshape(SEGS // 2, 2, FH // SEGS, 2 * WIDE)
    for side in range(2):
        rterm[side] = term[:, side]
        rlow[side] = term[:, side].astype(BF)
    pair.start()
    own_tile(0)
    own_tile(1)
    summed()
    own_tile(2)
    own_tile(3)
    gh = finished()

    for h in range(HEADS):
        gsb[h * COLS : (h + 1) * COLS] = (
            tn(gh, picked[:, head(h)]).astype(BF).reshape(COLS, PIECE, DK)
        )

    @pl.loop(1, SEGS)
    def _(d):
        gs_copy(lax.rem(me + d, SEGS), me).start()

    own_gs = pltpu.make_async_copy(gsb.at[slot(me)], gs_all.at[me], loc.at[3])
    own_gs.start()
    for o in (1, 2):
        stat_copy(o).wait()
    for copy in rows_near:
        copy.wait_recv()
    far_tile(1, 0)
    far_tile(2, 0)
    pair.wait()
    rbuf[...] = (rterm[core] + rpair[...].astype(F32)).astype(BF)
    far_tile(1, 1)

    @pl.loop(1, SEGS // 2)
    def _(d):
        r_copy(d).start()

    own_r = pltpu.make_async_copy(rbuf.at[chip], rall.at[chip], loc.at[4])
    own_r.start()
    far_tile(2, 1)
    far_tile(1, 2)
    far_tile(2, 2)

    own_gs.wait()
    own_r.wait()

    @pl.loop(1, SEGS)
    def _(d):
        src = lax.rem(me + SEGS - d, SEGS)
        gs_copy(src, src).wait_recv()

    state[...] = jnp.zeros((PIECE, DK), F32)

    @pl.loop(0, SEGS)
    def _(i):
        t = SEGS - 1 - i
        old = state[...]
        gout[t] = old.astype(BF)
        state[...] = step(old, er_all, t, gs_all[t])

    @pl.loop(1, SEGS)
    def _(d):
        g_copy(lax.rem(me + d, SEGS), me).start()

    own_g = pltpu.make_async_copy(gout.at[me], gt.at[slot(me)], loc.at[5])
    own_g.start()
    far_tile(1, 3)
    far_tile(2, 3)

    onehot = (
        lax.broadcasted_iota(jnp.int32, (SEG, NM), 0) == pos[...]
    ).astype(F32).astype(BF)
    for h in range(HEADS):
        m_h = mt[h * COLS : (h + 1) * COLS].reshape(FH, DK)
        grad_picked = nn(gh, m_h).astype(BF)
        out_q[:, head(h)] += nn(onehot, grad_picked)
    shipped = [
        pltpu.make_async_copy(out_v, ship_v, ship.at[0]),
        pltpu.make_async_copy(out_q, ship_q, ship.at[1]),
    ]
    for copy in shipped:
        copy.start()

    own_g.wait()

    @pl.loop(1, SEGS)
    def _(d):
        to = lax.rem(me + d, SEGS)
        gs_copy(to, me).wait_send()
        g_copy(to, me).wait_send()
        g_copy(to, to).wait_recv()

    def t_copy(d):
        to = lax.rem(my + d, PEERS)
        return remote(tparts.at[to], tparts.at[PEERS + d], s_t.at[d], r_t.at[d], {"head": to})

    for d in (1, 2, 3, 0):
        to = lax.rem(my + d, PEERS)
        term = jnp.zeros((SEG, DK), F32)
        for h in range(HEADS):
            rows = gt[pl.ds(h * COLS + 2 * to, 2)].reshape(DK, DK)
            term += nt(kk[:, head(h)], rows)
        tparts[to] = (term * (1.0 / SEG)).astype(BF)
        if d:
            t_copy(d).start()

    for h in range(HEADS):
        g_h = gt[h * COLS : (h + 1) * COLS].reshape(FH, DK)
        m_h = mt[h * COLS : (h + 1) * COLS].reshape(FH, DK)
        both = (tn(g_h, m_h) + tn(m_h, g_h)).astype(BF)
        out_k[:, head(h)] += nn(zz[...], g_h) * (1.0 / SEG) - nn(kk[:, head(h)], both) * (
            rate[0, h] / SEG
        )

    @pl.loop(1, SEGS // 2)
    def _(d):
        r_copy(d).wait()

    out_r[...] = jnp.sum(rall[...].astype(F32), axis=0)

    for d in range(1, PEERS):
        t_copy(d).wait()
    grad = tparts[my].astype(F32)
    for d in range(1, PEERS):
        grad += tparts[PEERS + d].astype(F32)
    out_z[...] = grad
    for d in range(1, 4):
        er_copy(mx, lax.rem(mx + d, 4)).wait_send()
        over_z(d).wait_send()
    for d in range(4):
        over_core(d, core).wait_send()
    for copy in far + keys_near + rows_near:
        copy.wait_send()
    for copy in shipped:
        copy.wait()


def finish_kernel(*refs):
    count = len(refs) // 3
    arrays, (load, store) = refs[: 2 * count], refs[3 * count :]
    held = refs[2 * count : 3 * count]
    loads, stores = [], []
    for i in range(count):
        half = arrays[i].shape[0] // 2
        for part in range(2):
            rows = pl.ds(part * half, half)
            slot_of = 2 * i + part
            loads.append(pltpu.make_async_copy(arrays[i].at[rows], held[i].at[rows], load.at[slot_of]))
            stores.append(
                pltpu.make_async_copy(held[i].at[rows], arrays[count + i].at[rows], store.at[slot_of])
            )
    for copy in loads:
        copy.start()
    for first, then in zip(loads, stores):
        first.wait()
        then.start()
    for copy in stores:
        copy.wait()


def shape(dims, kind):
    return jax.ShapeDtypeStruct(dims, kind)


def dma(*dims):
    return pltpu.SemaphoreType.DMA(dims)


def on_device(
    queries, key_rows, value_rows, targets, readout, retain, learn_rate, allowed, positions, grad_out
):
    block = (SEG, WIDE)
    segment = lax.axis_index("ctx")
    row = lax.dynamic_slice(allowed, (segment, 0), (1, 2))
    reach = lax.broadcasted_iota(jnp.int32, (1, 2), 1) < segment
    bias = jnp.where((row == 1) & reach, 0.0, NEG).astype(F32)
    results = (
        shape(block, F32),
        shape(block, F32),
        shape(block, F32),
        shape((SEG, FH // PEERS), F32),
        shape((FH // SEGS, 2 * WIDE), F32),
    )
    sums = [
        pltpu.VMEM((PEERS, NM, FH // PEERS), F32),
        pltpu.VMEM((PEERS, NM, FH // PEERS), F32),
        pltpu.VMEM((PEERS, NM, FH // PEERS), BF),
    ]
    low_pieces = pltpu.VMEM((SEGS, PIECE, DK), BF)
    terms = (SEGS // 2, FH // SEGS, 2 * WIDE)
    outs = pl.pallas_call(
        whole_kernel,
        out_shape=results,
        in_specs=[SM, SM, SM] + [VM] * 4 + [ANY] * 3,
        out_specs=(ANY, VM, ANY, VM, VM),
        scratch_shapes=[pltpu.VMEM(block, F32)] * 2
        + [pltpu.VMEM(block, BF)] * 10
        + [
            pltpu.VMEM((FH, 2 * WIDE), BF),
            pltpu.VMEM((HEADS, DK + ROWS_R, DK), BF),
            low_pieces,
            pltpu.VMEM((NM, WIDE), BF),
            pltpu.VMEM((NM, FH), BF),
            pltpu.VMEM((NM, 2 * WIDE), BF),
            pltpu.VMEM((SEGS, DK + ROWS_R, DK), BF),
            low_pieces,
            pltpu.VMEM((SEGS, PIECE, DK), STATE),
            pltpu.VMEM((SEGS, PIECE, DK), STATE),
            low_pieces,
        ]
        + sums
        + sums
        + [
            pltpu.VMEM((PEERS, NM, FH // PEERS), F32),
            pltpu.VMEM((PIECE, DK), F32),
            pltpu.VMEM((NM, 2 * WIDE), BF),
            pltpu.VMEM((8 * HEADS, SEG), F32),
            pltpu.VMEM((HEADS, SEG, 3 * SEG + NM), BF),
            pltpu.VMEM((HEADS, SEG, SEG), BF),
            low_pieces,
            low_pieces,
            low_pieces,
            low_pieces,
            pltpu.VMEM((2,) + terms, F32),
            pltpu.VMEM((2,) + terms, BF),
            pltpu.VMEM(terms, BF),
            pltpu.VMEM(terms, BF),
            pltpu.VMEM(terms, BF),
            pltpu.VMEM((2 * PEERS, SEG, FH // PEERS), BF),
            pltpu.VMEM((2, 8 * HEADS, SEG), F32),
            dma(4), dma(4), dma(SEGS), dma(SEGS), dma(SEGS), dma(SEGS),
            dma(8), dma(8), dma(2 * PEERS), dma(2 * PEERS), dma(8), dma(8),
            dma(SEGS), dma(SEGS), dma(SEGS), dma(SEGS), dma(SEGS // 2), dma(SEGS // 2),
            dma(2 * PEERS), dma(2 * PEERS), dma(PEERS), dma(PEERS), dma(2), dma(2), dma(6), dma(3), dma(2),
        ],
        compiler_params=pltpu.CompilerParams(
            collective_id=0, has_side_effects=True, vmem_limit_bytes=LIMIT
        ),
        name="whole",
    )(
        retain, learn_rate, bias, queries, key_rows, targets, positions, value_rows, grad_out, readout,
    )
    return pl.pallas_call(
        finish_kernel,
        out_shape=results,
        in_specs=[ANY] * 5,
        out_specs=(ANY,) * 5,
        scratch_shapes=[pltpu.VMEM(out.shape, F32) for out in results] + [dma(10), dma(10)],
        compiler_params=pltpu.CompilerParams(vmem_limit_bytes=LIMIT),
        name="finish",
    )(*outs)


def solution(mesh):
    return jax.shard_map(
        on_device,
        mesh=mesh,
        in_specs=(
            P("ctx", "head"),
            P("ctx", "head"),
            P("ctx", "head"),
            P("ctx", None),
            P(None, "head"),
            P("ctx", "head"),
            P("ctx", "head"),
            P(),
            P("ctx", None),
            P("ctx", "head"),
        ),
        out_specs=(P("ctx", "head"),) * 5,
        check_vma=False,
    )
```
